512 devices in a mesh: dp: 16 (over x, z_hi, core), ctx: 32 (over z_lo, y).
Axes of the slice: x: 4, y: 8, z: 8 (z_hi: 2, z_lo: 4; z = z_hi * 4 + z_lo), core: 2. Of those that a mesh axis runs over, the one named last changes fastest.
Arguments:
- queries: bfloat16 [16, 4096, 1024], P('dp', 'ctx'), may hold values from -1.75 to 1.75
- keys: bfloat16 [16, 4096, 1024], P('dp', 'ctx'), may hold values from -1.8 to 1.8
- values: bfloat16 [16, 4096, 1024], P('dp', 'ctx'), may hold values from -3 to 3
- out_grad: bfloat16 [16, 4096, 1024], P('dp', 'ctx'), may hold values from -1.5 to 1.5
- layer_grad: bfloat16 [16, 4096, 768], P('dp', 'ctx'), may hold values from -6 to 6
- norm_gain: float32 [1024], replicated, may hold values from 0.1 to 1.9
- decay_rates: float32 [8], replicated, as said below
- doc_lengths: int32 [16, 4], P('dp'), may hold values from 1 to 2048, 4096 in all within a row
Outputs:
- query_grad: bfloat16 [16, 4096, 1024], P('dp', 'ctx')
- key_grad: bfloat16 [16, 4096, 1024], P('dp', 'ctx')
- value_grad: bfloat16 [16, 4096, 1024], P('dp', 'ctx')
- proj_grad: float32 [1024, 768], P(('dp', 'ctx'))
The draws below stay inside these ranges and needn't reach their ends.
Inputs may be any that keep to these rules, and one draw needn't show every extreme that they name: `decay_rates`: positive rates; a head's state is multiplied by exp(-rate) per position. `doc_lengths`: each row sums to 4096; the longest document has exactly 2048 positions.
All inputs are finite; a program needn't handle non-finite values.
Results may differ from the reference program's by a relative error of at most 0.0029.
Values sent between devices are 32-bit elements; how exact they have to be, the bound alone decides.
A program may use at most 128 MiB of HBM per device.

```python
import math
import jax
import jax.numpy as jnp
import numpy as np
from jax import lax

HEADS = 8
DH = 128
TB = 128
NDOC = 4
BUCKET = 768
LEN = 4096
SEQS = 16
HD = 1024
MOSTLEN = 2048
TOKENS = 65536


def head_rates(key):
    rate_key = jax.random.fold_in(key, 11)
    chooser_key, fast_key, middle_key, slow_key = jax.random.split(rate_key, 4)
    chooser = jax.random.uniform(chooser_key, (HEADS,), jnp.float32)
    fast_rate = jnp.exp(jax.random.uniform(fast_key, (HEADS,), jnp.float32, math.log(1.0 / 50.0), math.log(1.0 / 30.0)))
    middle_rate = jnp.exp(jax.random.uniform(middle_key, (HEADS,), jnp.float32, math.log(0.005), math.log(0.015)))
    slow_rate = jnp.exp(jax.random.uniform(slow_key, (HEADS,), jnp.float32, math.log(0.3 / LEN), math.log(2.3 / LEN)))
    fast_share = 0.25
    middle_share = 0.5
    return jnp.where(chooser < fast_share, fast_rate, jnp.where(chooser < middle_share, middle_rate, slow_rate))


def block_gains(key):
    gain_key = jax.random.fold_in(key, 23)
    levels = jax.random.uniform(gain_key, (SEQS, LEN // TB), jnp.float32, -3.0, 0.0)
    return jnp.repeat(jnp.exp(levels), TB, axis=1)[:, :, None]


def unit_noise(key, shape):
    noise_draw = jax.random.normal(key, shape, jnp.float32)
    return jnp.clip(noise_draw, -6.0, 6.0)


def draw_decay_rates(key, part):
    return head_rates(key)


def draw_keys(key, part):
    noise_draw = unit_noise(jax.random.fold_in(key, 31), (SEQS, LEN, HD))
    return (0.3 * block_gains(key) * noise_draw).astype(jnp.bfloat16)


def draw_values(key, part):
    rates = head_rates(key)
    head_scales = 0.5 * jnp.sqrt(jnp.maximum(rates, 4.0 / LEN) * 30.0)
    feature_scales = jnp.repeat(head_scales, DH)
    noise_draw = unit_noise(jax.random.fold_in(key, 37), (SEQS, LEN, HD))
    return (feature_scales * block_gains(key) * noise_draw).astype(jnp.bfloat16)


def block_scale(own_key, shape, shards, least, high):
    gain, own = 1.0, jax.random.fold_in(own_key, 6)
    for axis_at, shards_of in shards:
        draws = jnp.exp(jax.random.uniform(jax.random.fold_in(own, axis_at), (shards_of,), jnp.float32, least / len(shards), high / len(shards)))
        gain = gain * jnp.repeat(draws, shape[axis_at] // shards_of).reshape([-1 if axis == axis_at else 1 for axis in range(len(shape))])
    return gain


def split_up(count, total, bound, skew):
    loads = [(1 << 20) // math.isqrt(standing ** skew) + 1 for standing in range(2, count + 1)]
    rest, given = total - bound - (count - 1), [1] * (count - 1)
    while rest > 0:
        candidates = [i for i in range(count - 1) if given[i] < bound]
        pool, left = sum([loads[i] for i in candidates]), rest
        for i in candidates:
            more = min(bound - given[i], max(1, left * loads[i] // pool), rest)
            given[i] = given[i] + more
            rest = rest - more
    return np.array([bound] + given)


def ragged(stream_key, number_of, total, limit, slope):
    if number_of == 2:
        one = jax.random.randint(stream_key, (), max(1, total - limit), min(limit, total - 1) + 1)
        return jnp.stack([one, total - one])
    tallies = jnp.asarray(split_up(number_of, total, limit, slope), jnp.int32)
    twos = (number_of - 1) // 2
    giver, receiver = tallies[1:1 + 2 * twos:2], tallies[2:2 + 2 * twos:2]
    margin = jnp.minimum(giver - 1, limit - receiver)
    passed = jax.random.randint(jax.random.fold_in(stream_key, 1), (twos,), 0, 1 << 20) % (margin + 1)
    tallies = tallies.at[1:1 + 2 * twos:2].set(giver - passed).at[2:2 + 2 * twos:2].set(receiver + passed)
    return tallies[jax.random.permutation(jax.random.fold_in(stream_key, 2), number_of)]


def normal_values(rng, extent, scale, limit, cuts=(), kind=jnp.bfloat16):
    result = jax.random.normal(rng, extent, jnp.float32) * scale
    if len(cuts) > 0:
        result = block_scale(rng, extent, cuts, -0.22, 0.18) * result
    return jnp.clip(result, min=-limit, max=limit).astype(kind)


def setup_inputs(seed: int = 0) -> dict:
    seeds = jax.random.split(jax.random.key(seed), 9)
    queries = normal_values(seeds[0], (SEQS, LEN, HD), 0.3, 1.75, ((0, 16), (1, 32)))
    keys = draw_keys(jax.random.fold_in(seeds[8], 71), 0)
    values = draw_values(jax.random.fold_in(seeds[8], 71), 0)
    out_grad = normal_values(seeds[3], (SEQS, LEN, HD), 0.25, 1.5, ((0, 16), (1, 32)))
    layer_grad = normal_values(seeds[4], (SEQS, LEN, BUCKET), 1.0, 6.0, ((0, 16), (1, 32)))
    norm_gain = jnp.clip(1.0 + 0.18 * jax.random.normal(seeds[5], (HD,), jnp.float32), 0.1, 1.9)
    decay_rates = draw_decay_rates(jax.random.fold_in(seeds[8], 71), 0)
    doc_lengths = jax.vmap(lambda own: ragged(own, NDOC, LEN, MOSTLEN, 2))(jax.random.split(seeds[7], SEQS)).reshape((SEQS, NDOC)).astype(jnp.int32)
    return dict(queries=queries, keys=keys, values=values, out_grad=out_grad, layer_grad=layer_grad, norm_gain=norm_gain, decay_rates=decay_rates, doc_lengths=doc_lengths)


highest = lax.Precision.HIGHEST
norm_eps = 1e-06

def doc_index(positions, lengths):
    bounds = jnp.cumsum(lengths).astype(jnp.int32)[:-1]
    return lax.optimization_barrier(jnp.sum((positions[..., None] >= bounds).astype(jnp.int32), axis=-1)).astype(jnp.int32)

def decay_tables(decay_rate, doc_ids, prev_id, last_id):
    length = doc_ids.shape[0]
    offsets = jnp.arange(length, dtype=jnp.float32)
    distance = offsets[:, None] - offsets[None, :]
    same_doc = (doc_ids[:, None] == doc_ids[None, :]) & (distance >= 0.0)
    decay_mask = jnp.where(same_doc[None], jnp.exp(-decay_rate[:, None, None] * jnp.maximum(distance, 0.0)[None]), 0.0)
    entry_decay = jnp.where((doc_ids == prev_id)[None, :], jnp.exp(-decay_rate[:, None] * offsets[None, :]), 0.0)
    exit_decay = jnp.where((doc_ids == last_id)[None, :], jnp.exp(-decay_rate[:, None] * (length - offsets)[None, :]), 0.0)
    carry_all = jnp.where(last_id == prev_id, jnp.exp(-decay_rate * length), 0.0)
    return (decay_mask, entry_decay, exit_decay, carry_all)

def block_summary(query_rows, key_rows, value_rows, grad_rows, tables):
    decay_mask, entry_decay, exit_decay, carry_all = tables
    keys_out = key_rows * exit_decay.T[:, :, None]
    local_state = jnp.einsum('jhd,jhe->hde', keys_out, value_rows, precision=highest)
    queries_in = query_rows * entry_decay.T[:, :, None]
    state_pull = jnp.einsum('ihd,ihe->hde', queries_in, grad_rows, precision=highest)
    return (carry_all, local_state, state_pull)

def block_outputs(query_rows, key_rows, value_rows, grad_rows, tables, state_in, state_grad):
    decay_mask, entry_decay, exit_decay, carry_all = tables
    entry_t = entry_decay.T[:, :, None]
    exit_t = exit_decay.T[:, :, None]
    scores = jnp.einsum('ihd,jhd->hij', query_rows, key_rows, precision=highest) * decay_mask
    attention = jnp.einsum('hij,jhe->ihe', scores, value_rows, precision=highest)
    attention = attention + entry_t * jnp.einsum('ihd,hde->ihe', query_rows, state_in, precision=highest)
    grads = jnp.einsum('ihe,jhe->hij', grad_rows, value_rows, precision=highest) * decay_mask
    query_grad = jnp.einsum('hij,jhd->ihd', grads, key_rows, precision=highest)
    query_grad = query_grad + entry_t * jnp.einsum('ihe,hde->ihd', grad_rows, state_in, precision=highest)
    key_grad = jnp.einsum('hij,ihd->jhd', grads, query_rows, precision=highest)
    key_grad = key_grad + exit_t * jnp.einsum('jhe,hde->jhd', value_rows, state_grad, precision=highest)
    value_grad = jnp.einsum('hij,ihe->jhe', scores, grad_rows, precision=highest)
    value_grad = value_grad + exit_t * jnp.einsum('jhd,hde->jhe', key_rows, state_grad, precision=highest)
    return (attention, query_grad, key_grad, value_grad)

def reference(queries, keys, values, out_grad, layer_grad, norm_gain, decay_rates, doc_lengths):
    block_count = LEN // TB
    grad_scale = 1.0 / math.sqrt(TOKENS)

    def one_sequence(inputs):
        query_seq, key_seq, value_seq, grad_seq, layer_seq, lengths = inputs

        def split_heads(array):
            return array.astype(jnp.float32).reshape(block_count, TB, HEADS, DH)
        query_rows = split_heads(query_seq)
        key_rows = split_heads(key_seq)
        value_rows = split_heads(value_seq)
        grad_rows = split_heads(grad_seq)
        positions = jnp.arange(LEN, dtype=jnp.int32).reshape(block_count, TB)
        doc_ids = doc_index(positions, lengths)
        prev_ids = doc_index(jnp.arange(block_count, dtype=jnp.int32) * TB - 1, lengths)
        last_ids = doc_ids[:, -1]
        tables = jax.vmap(decay_tables, in_axes=(None, 0, 0, 0))(decay_rates, doc_ids, prev_ids, last_ids)
        carry_all, local_state, state_pull = jax.vmap(block_summary)(query_rows, key_rows, value_rows, grad_rows, tables)

        def advance(state_now, element):
            return (element[0][:, None, None] * state_now + element[1], state_now)
        empty = jnp.zeros((HEADS, DH, DH), jnp.float32)
        states_in = lax.scan(advance, empty, (carry_all, local_state))[1]
        state_grads = lax.scan(advance, empty, (carry_all, state_pull), reverse=True)[1]
        attention, query_grad, key_grad, value_grad = jax.vmap(block_outputs)(query_rows, key_rows, value_rows, grad_rows, tables, states_in, state_grads)
        attention = attention.reshape(LEN, HD)
        normed = (attention * lax.rsqrt(lax.optimization_barrier(jnp.mean(attention * attention, axis=-1, keepdims=True)) + norm_eps) * norm_gain).astype(jnp.bfloat16)
        term = jnp.dot(normed.astype(jnp.float32).T, layer_seq.astype(jnp.float32), precision=highest)
        return (term, query_grad.reshape(LEN, HD).astype(jnp.bfloat16), key_grad.reshape(LEN, HD).astype(jnp.bfloat16), value_grad.reshape(LEN, HD).astype(jnp.bfloat16))
    terms, query_grad, key_grad, value_grad = lax.map(one_sequence, (queries, keys, values, out_grad, layer_grad, doc_lengths))
    proj_grad = lax.optimization_barrier(jnp.sum(terms, axis=0)) * grad_scale
    return (query_grad, key_grad, value_grad, proj_grad)
```

```python
import functools
import math

import jax
import jax.numpy as jnp
from jax import lax
from jax.experimental import pallas as pl
from jax.experimental.pallas import tpu as pltpu
from jax.sharding import PartitionSpec as P

norm_eps = 1e-06
HEADS, WIDTH, ROWS = 8, 128, 128
NX, NZ, NY, NZL = 4, 8, 8, 4
MESH = pl.DeviceIdType.MESH
f32, bf16 = jnp.float32, jnp.bfloat16
VMEM_SPEC = pl.BlockSpec(memory_space=pltpu.VMEM)
SMEM_SPEC = pl.BlockSpec(memory_space=pltpu.SMEM)


def split(value):
    high = value.astype(bf16)
    return high, (value - high.astype(f32)).astype(bf16)


def matmul(a, b, dims):
    return lax.dot_general(a, b, (dims, ((), ())), preferred_element_type=f32)


NN, NT, TN = ((1,), (0,)), ((1,), (1,)), ((0,), (0,))


def doc_bounds(len_ref):
    first = len_ref[0, 0]
    second = first + len_ref[0, 1]
    return first, second, second + len_ref[0, 2]


def doc_of(positions, bounds):
    return sum((positions >= bound).astype(jnp.int32) for bound in bounds)


def doc_of_scalar(position, bounds):
    return sum(jnp.where(position >= bound, 1, 0) for bound in bounds)


def edge_tables(base, bounds):
    offsets = lax.broadcasted_iota(jnp.int32, (ROWS, WIDTH), 0)
    docs = doc_of(base + offsets, bounds)
    entering = docs == doc_of_scalar(base - 1, bounds)
    leaving = docs == doc_of_scalar(base + ROWS - 1, bounds)
    return offsets.astype(f32), entering, leaving


def summary_kernel(q_ref, k_ref, v_ref, g_ref, rate_ref, len_ref, state_ref, pull_ref, carry_ref):
    ctx = lax.axis_index("ctx")
    bounds = doc_bounds(len_ref)
    offsets, entering, leaving = edge_tables(ctx * ROWS, bounds)
    for h in range(HEADS):
        cols = pl.ds(h * WIDTH, WIDTH)
        rate = rate_ref[h]
        entry = jnp.where(entering, jnp.exp(-rate * offsets), 0.0)
        leave = jnp.where(leaving, jnp.exp(-rate * (ROWS - offsets)), 0.0)
        high, low = split(k_ref[:, cols].astype(f32) * leave)
        v = v_ref[:, cols]
        state_ref[h] = matmul(high, v, TN) + matmul(low, v, TN)
        high, low = split(q_ref[:, cols].astype(f32) * entry)
        g = g_ref[:, cols]
        pull_ref[h] = matmul(high, g, TN) + matmul(low, g, TN)
    group, own = ctx // NY, lax.rem(ctx, NY)
    rate = rate_ref[own]

    def carry(first, blocks):
        start = first * ROWS
        whole = doc_of_scalar(start - 1, bounds) == doc_of_scalar(start + blocks * ROWS - 1, bounds)
        decay = jnp.exp(jnp.full((1, WIDTH), -rate * float(blocks * ROWS), f32))
        return jnp.where(whole, decay, 0.0)

    for j in range(NY):
        carry_ref[pl.ds(j, 1), :] = carry(group * NY + j, 1)
    carry_ref[pl.ds(8, 1), :] = carry((group - 1) * NY, NY)
    carry_ref[pl.ds(9, 1), :] = carry((group + 1) * NY, NY)


def scan_kernel(
    state_ref, pull_ref, carry_ref, in_ref, grad_ref,
    state_buf, pull_buf, in_buf, grad_buf, total_buf, group_buf,
    out_send, out_recv, back_send, back_recv, group_send, group_recv,
):
    dp, ctx = lax.axis_index("dp"), lax.axis_index("ctx")
    z, y = ctx // NY, lax.rem(ctx, NY)
    barrier = pltpu.get_barrier_semaphore()

    def at_y(k):
        return (dp, z * NY + lax.rem(y + k, NY))

    for k in range(1, NY):
        pl.semaphore_signal(barrier, inc=1, device_id=at_y(k), device_id_type=MESH)
    for k in range(1, NZL):
        there = (dp, lax.rem(z + k, NZL) * NY + y)
        pl.semaphore_signal(barrier, inc=1, device_id=there, device_id_type=MESH)
    pl.semaphore_wait(barrier, NY - 1 + NZL - 1)

    def send(src, dst, send_sem, recv_sem, device):
        return pltpu.make_async_remote_copy(
            src_ref=src, dst_ref=dst, send_sem=send_sem, recv_sem=recv_sem,
            device_id=device, device_id_type=MESH,
        )

    out_copies = []
    for d, (src, buf) in enumerate(((state_ref, state_buf), (pull_ref, pull_buf))):
        for k in range(1, NY):
            copy = send(
                src.at[lax.rem(y + k, NY)], buf.at[k], out_send.at[d, k], out_recv.at[d, k], at_y(k)
            )
            copy.start()
            out_copies.append(copy)

    def carry(j):
        return carry_ref[pl.ds(j, 1), :]

    def slot(j):
        return lax.rem(y - j + NY, NY)

    orders = (tuple(range(NY)), tuple(reversed(range(NY))))
    steps = (1, -1)

    def group_copy(d, far):
        there = (dp, (z + steps[d] * far) * NY + y)
        return send(
            total_buf.at[d], group_buf.at[d, far - 1],
            group_send.at[d, far - 1], group_recv.at[d, far - 1], there,
        )

    for d, (src, buf) in enumerate(((state_ref, state_buf), (pull_ref, pull_buf))):
        buf[0] = src[y]
        for copy in out_copies[d * (NY - 1):(d + 1) * (NY - 1)]:
            copy.wait_recv()
        total = jnp.zeros((WIDTH, WIDTH), f32)
        for j in orders[d]:
            total = carry(j) * total + buf[slot(j)]
        total_buf[d] = total
        for far in (1, 2):
            has_target = z + far < NZL if d == 0 else z - far >= 0

            @pl.when(has_target)
            def _():
                group_copy(d, far).start()

    back_copies = []
    for d, (buf, back, result) in enumerate(((state_buf, in_buf, in_ref), (pull_buf, grad_buf, grad_ref))):
        for far in (1, 2):
            has_source = z - far >= 0 if d == 0 else z + far < NZL

            @pl.when(has_source)
            def _():
                group_copy(d, far).wait_recv()

            @pl.when(jnp.logical_not(has_source))
            def _():
                group_buf[d, far - 1] = jnp.zeros((WIDTH, WIDTH), f32)

        now = group_buf[d, 0] + carry(8 + d) * group_buf[d, 1]
        for j in orders[d]:
            back[j] = now
            if j != orders[d][-1]:
                now = carry(j) * now + buf[slot(j)]
        for k in range(1, NY):
            copy = send(
                back.at[lax.rem(y + k, NY)], result.at[y],
                back_send.at[d, k], back_recv.at[d, k], at_y(k),
            )
            copy.start()
            back_copies.append((d, k, copy))
        result[y] = back[y]

    for d, k, copy in back_copies:
        result = (in_ref, grad_ref)[d]
        arrived = send(
            in_buf.at[0], result.at[lax.rem(y - k + NY, NY)],
            back_send.at[d, k], back_recv.at[d, k], at_y(k),
        )
        arrived.wait_recv()
    for d in range(2):
        for far in (1, 2):
            has_target = z + far < NZL if d == 0 else z - far >= 0

            @pl.when(has_target)
            def _():
                group_copy(d, far).wait_send()
    for copy in out_copies:
        copy.wait_send()
    for _, _, copy in back_copies:
        copy.wait_send()


def outputs_kernel(
    q_ref, k_ref, v_ref, g_ref, layer_ref, gain_ref, rate_ref, len_ref, in_ref, grad_ref,
    dq_ref, dk_ref, dv_ref, product_ref, attention_buf, normed_buf,
):
    base = lax.axis_index("ctx") * ROWS
    bounds = doc_bounds(len_ref)
    offsets, entering, leaving = edge_tables(base, bounds)
    rows = lax.broadcasted_iota(jnp.int32, (ROWS, ROWS), 0)
    columns = lax.broadcasted_iota(jnp.int32, (ROWS, ROWS), 1)
    same = (doc_of(base + rows, bounds) == doc_of(base + columns, bounds)) & (rows >= columns)
    distance = jnp.maximum(rows - columns, 0).astype(f32)
    for h in range(HEADS):
        cols = pl.ds(h * WIDTH, WIDTH)
        rate = rate_ref[h]
        q, k, v, g = q_ref[:, cols], k_ref[:, cols], v_ref[:, cols], g_ref[:, cols]
        mask = jnp.where(same, jnp.exp(-rate * distance), 0.0)
        entry = jnp.where(entering, jnp.exp(-rate * offsets), 0.0)
        leave = jnp.where(leaving, jnp.exp(-rate * (ROWS - offsets)), 0.0)
        s_high, s_low = split(matmul(q, k, NT) * mask)
        d_high, d_low = split(matmul(g, v, NT) * mask)
        in_high, in_low = split(in_ref[h])
        grad_high, grad_low = split(grad_ref[h])
        attention = matmul(s_high, v, NN) + matmul(s_low, v, NN)
        attention += entry * (matmul(q, in_high, NN) + matmul(q, in_low, NN))
        attention_buf[:, cols] = attention
        dq = matmul(d_high, k, NN) + matmul(d_low, k, NN)
        dq += entry * (matmul(g, in_high, NT) + matmul(g, in_low, NT))
        dq_ref[:, cols] = dq.astype(bf16)
        dk = matmul(d_high, q, TN) + matmul(d_low, q, TN)
        dk += leave * (matmul(v, grad_high, NT) + matmul(v, grad_low, NT))
        dk_ref[:, cols] = dk.astype(bf16)
        dv = matmul(s_high, g, TN) + matmul(s_low, g, TN)
        dv += leave * (matmul(k, grad_high, NN) + matmul(k, grad_low, NN))
        dv_ref[:, cols] = dv.astype(bf16)
    attention = attention_buf[...]
    mean = jnp.mean(attention * attention, axis=-1, keepdims=True)
    normed_buf[...] = (attention * lax.rsqrt(mean + norm_eps) * gain_ref[...]).astype(bf16)
    for h in range(HEADS):
        cols = pl.ds(h * WIDTH, WIDTH)
        product_ref[cols, :] = matmul(normed_buf[:, cols], layer_ref[...], TN)


def reduce_kernel(
    scale, p_ref, out_ref, core_buf, a_buf, x_buf, b_buf, z_buf, c_buf, y_buf,
    core_send, core_recv, x_send, x_recv, z_send, z_recv, y_send, y_recv,
):
    dp, ctx = lax.axis_index("dp"), lax.axis_index("ctx")
    x, z_high, core = dp // 4, lax.rem(dp // 2, 2), lax.rem(dp, 2)
    z, y = z_high * 4 + ctx // NY, lax.rem(ctx, NY)
    twin = (dp + 1 - 2 * core, ctx)

    def at_x(k):
        return (lax.rem(x + k, NX) * 4 + lax.rem(dp, 4), ctx)

    def at_z(k):
        there = lax.rem(z + k, NZ)
        return (x * 4 + there // 4 * 2 + core, lax.rem(there, 4) * NY + y)

    def at_y(k):
        return (dp, ctx - y + lax.rem(y + k, NY))

    barrier = pltpu.get_barrier_semaphore()
    pl.semaphore_signal(barrier, inc=1, device_id=twin, device_id_type=MESH)
    for at, count in ((at_x, NX), (at_z, NZ), (at_y, NY)):
        for k in range(1, count):
            pl.semaphore_signal(barrier, inc=1, device_id=at(k), device_id_type=MESH)
    pl.semaphore_wait(barrier, NX + NZ + NY - 2)

    def send(src, dst, sems, k, device):
        copy = pltpu.make_async_remote_copy(
            src_ref=src, dst_ref=dst, send_sem=sems[0].at[k], recv_sem=sems[1].at[k],
            device_id=device, device_id_type=MESH,
        )
        copy.start()
        return copy

    order = tuple(range(1, NX)) + (0,)
    core_copies, copies = [], []
    for k in order:
        there = lax.rem(x + k, NX)
        core_copies.append(
            send(p_ref.at[there, :, 1 - core], core_buf.at[k], (core_send, core_recv), k, twin)
        )
    x_copies = []
    for k, copy in zip(order, core_copies):
        copy.wait_recv()
        a_buf[k] = p_ref[lax.rem(x + k, NX), :, core] + core_buf[k]
        if k:
            x_copies.append(send(a_buf.at[k], x_buf.at[k], (x_send, x_recv), k, at_x(k)))
    total = a_buf[0]
    for k, copy in enumerate(x_copies, 1):
        copy.wait_recv()
        total = total + x_buf[k]
    b_buf[...] = total.reshape(b_buf.shape)
    z_copies = [
        send(b_buf.at[lax.rem(z + k, NZ)], z_buf.at[k], (z_send, z_recv), k, at_z(k))
        for k in range(1, NZ)
    ]
    total = b_buf[z]
    for k, copy in enumerate(z_copies, 1):
        copy.wait_recv()
        total = total + z_buf[k]
    for j in range(NY):
        c_buf[j] = total[2 * j:2 * j + 2, :]
    y_copies = [
        send(c_buf.at[lax.rem(y + k, NY)], y_buf.at[k], (y_send, y_recv), k, at_y(k))
        for k in range(1, NY)
    ]
    total = c_buf[y]
    for k, copy in enumerate(y_copies, 1):
        copy.wait_recv()
        total = total + y_buf[k]
    out_ref[...] = total * scale
    for copy in core_copies + x_copies + z_copies + y_copies:
        copy.wait_send()


def on_device(queries, keys, values, out_grad, layer_grad, norm_gain, decay_rates, doc_lengths):
    rows, features, bucket = ROWS, HEADS * WIDTH, layer_grad.shape[2]
    scale = 1.0 / math.sqrt(rows * lax.axis_size("dp") * lax.axis_size("ctx"))
    q, k, v, g = (a.reshape(rows, features) for a in (queries, keys, values, out_grad))
    layer = layer_grad.reshape(rows, bucket)
    states = jax.ShapeDtypeStruct((HEADS, WIDTH, WIDTH), f32)
    heads_buf = pltpu.VMEM((HEADS, WIDTH, WIDTH), f32)
    state, pull, carry = pl.pallas_call(
        summary_kernel,
        out_shape=(states, states, jax.ShapeDtypeStruct((16, WIDTH), f32)),
        in_specs=[VMEM_SPEC] * 4 + [SMEM_SPEC] * 2,
        out_specs=(VMEM_SPEC,) * 3,
        name="summary",
    )(q, k, v, g, decay_rates, doc_lengths)
    state_in, state_grad = pl.pallas_call(
        scan_kernel,
        out_shape=(states, states),
        in_specs=[VMEM_SPEC] * 3,
        out_specs=(VMEM_SPEC,) * 2,
        scratch_shapes=[heads_buf] * 4
        + [pltpu.VMEM((2, WIDTH, WIDTH), f32), pltpu.VMEM((2, 2, WIDTH, WIDTH), f32)]
        + [pltpu.SemaphoreType.DMA((2, NY))] * 4
        + [pltpu.SemaphoreType.DMA((2, 2))] * 2,
        compiler_params=pltpu.CompilerParams(collective_id=0, has_side_effects=True),
        name="scan",
    )(state, pull, carry)
    grad_shape = jax.ShapeDtypeStruct((rows, features), bf16)
    query_grad, key_grad, value_grad, product = pl.pallas_call(
        outputs_kernel,
        out_shape=(grad_shape,) * 3 + (jax.ShapeDtypeStruct((features, bucket), f32),),
        in_specs=[VMEM_SPEC] * 6 + [SMEM_SPEC] * 2 + [VMEM_SPEC] * 2,
        out_specs=(VMEM_SPEC,) * 4,
        scratch_shapes=[pltpu.VMEM((rows, features), f32), pltpu.VMEM((rows, features), bf16)],
        name="outputs",
    )(q, k, v, g, layer, norm_gain.reshape(1, features), decay_rates, doc_lengths, state_in, state_grad)
    proj_grad = pl.pallas_call(
        functools.partial(reduce_kernel, scale),
        out_shape=jax.ShapeDtypeStruct((2, bucket), f32),
        in_specs=[VMEM_SPEC],
        out_specs=VMEM_SPEC,
        scratch_shapes=[
            pltpu.VMEM((NX, 2, 64, bucket), f32),
            pltpu.VMEM((NX, 2, 64, bucket), f32),
            pltpu.VMEM((NX, 2, 64, bucket), f32),
            pltpu.VMEM((NZ, 16, bucket), f32),
            pltpu.VMEM((NZ, 16, bucket), f32),
            pltpu.VMEM((NY, 2, bucket), f32),
            pltpu.VMEM((NY, 2, bucket), f32),
        ]
        + [pltpu.SemaphoreType.DMA((NX,))] * 4
        + [pltpu.SemaphoreType.DMA((NZ,))] * 2
        + [pltpu.SemaphoreType.DMA((NY,))] * 2,
        compiler_params=pltpu.CompilerParams(collective_id=1, has_side_effects=True),
        name="reduce",
    )(product.reshape(NX, 2, 2, 64, bucket))
    shape_out = (1, rows, features)
    return (
        query_grad.reshape(shape_out),
        key_grad.reshape(shape_out),
        value_grad.reshape(shape_out),
        proj_grad,
    )


def solution(mesh):
    block = P("dp", "ctx", None)
    return jax.shard_map(
        on_device,
        mesh=mesh,
        in_specs=(block,) * 5 + (P(), P(), P("dp", None)),
        out_specs=(block,) * 3 + (P(("dp", "ctx"), None),),
        check_vma=False,
    )
```

```python
import functools
import math

import jax
import jax.numpy as jnp
from jax import lax
from jax.experimental import pallas as pl
from jax.experimental.pallas import tpu as pltpu
from jax.sharding import PartitionSpec as P

norm_eps = 1e-06
HEADS, WIDTH, ROWS = 8, 128, 128
NX, NZ, NY, NZL = 4, 8, 8, 4
XCOLS = 512
MESH = pl.DeviceIdType.MESH
f32, bf16 = jnp.float32, jnp.bfloat16
VMEM_SPEC = pl.BlockSpec(memory_space=pltpu.VMEM)
SMEM_SPEC = pl.BlockSpec(memory_space=pltpu.SMEM)


def split(value):
    high = value.astype(bf16)
    return high, (value - high.astype(f32)).astype(bf16)


def matmul(a, b, dims):
    return lax.dot_general(a, b, (dims, ((), ())), preferred_element_type=f32)


NN, NT, TN = ((1,), (0,)), ((1,), (1,)), ((0,), (0,))


def doc_bounds(len_ref):
    first = len_ref[0, 0]
    second = first + len_ref[0, 1]
    return first, second, second + len_ref[0, 2]


def doc_of(positions, bounds):
    return sum((positions >= bound).astype(jnp.int32) for bound in bounds)


def doc_of_scalar(position, bounds):
    return sum(jnp.where(position >= bound, 1, 0) for bound in bounds)


def edge_tables(base, bounds):
    offsets = lax.broadcasted_iota(jnp.int32, (ROWS, WIDTH), 0)
    docs = doc_of(base + offsets, bounds)
    entering = docs == doc_of_scalar(base - 1, bounds)
    leaving = docs == doc_of_scalar(base + ROWS - 1, bounds)
    return offsets.astype(f32), entering, leaving


def summary_kernel(q_ref, k_ref, v_ref, g_ref, rate_ref, len_ref, state_ref, pull_ref, carry_ref):
    ctx = lax.axis_index("ctx")
    bounds = doc_bounds(len_ref)
    offsets, entering, leaving = edge_tables(ctx * ROWS, bounds)
    for h in range(HEADS):
        cols = pl.ds(h * WIDTH, WIDTH)
        rate = rate_ref[h]
        entry = jnp.where(entering, jnp.exp(-rate * offsets), 0.0)
        leave = jnp.where(leaving, jnp.exp(-rate * (ROWS - offsets)), 0.0)
        high, low = split(k_ref[:, cols].astype(f32) * leave)
        v = v_ref[:, cols]
        state_ref[h] = matmul(high, v, TN) + matmul(low, v, TN)
        high, low = split(q_ref[:, cols].astype(f32) * entry)
        g = g_ref[:, cols]
        pull_ref[h] = matmul(high, g, TN) + matmul(low, g, TN)
    group, own = ctx // NY, lax.rem(ctx, NY)
    rate = rate_ref[own]

    def carry(first, blocks):
        start = first * ROWS
        whole = doc_of_scalar(start - 1, bounds) == doc_of_scalar(start + blocks * ROWS - 1, bounds)
        decay = jnp.exp(jnp.full((1, WIDTH), -rate * float(blocks * ROWS), f32))
        return jnp.where(whole, decay, 0.0)

    for j in range(NY):
        carry_ref[pl.ds(j, 1), :] = carry(group * NY + j, 1)
    carry_ref[pl.ds(8, 1), :] = carry((group - 1) * NY, NY)
    carry_ref[pl.ds(9, 1), :] = carry((group + 1) * NY, NY)


def place():
    dp, ctx = lax.axis_index("dp"), lax.axis_index("ctx")
    return dp, ctx, ctx // NY, lax.rem(ctx, NY)


def send(src, dst, sems, at, device):
    return pltpu.make_async_remote_copy(
        src_ref=src, dst_ref=dst, send_sem=sems[0].at[at], recv_sem=sems[1].at[at],
        device_id=device, device_id_type=MESH,
    )


def started(copies):
    for copy in copies:
        copy.start()
    return copies


class Scan:
    def __init__(self, step, src, carry, result, bufs, out_sems, back_sems, group_sems):
        self.step, self.src, self.carry_ref, self.result = step, src, carry, result
        self.buf, self.back, self.total, self.group = bufs
        self.out_sems, self.back_sems, self.group_sems = out_sems, back_sems, group_sems
        self.dp, _, self.z, self.y = place()
        self.order = range(NY) if step > 0 else range(NY - 1, -1, -1)

    def at_y(self, k):
        return (self.dp, self.z * NY + lax.rem(self.y + k, NY))

    def carry(self, j):
        return self.carry_ref[pl.ds(j, 1), :]

    def block(self, j):
        return self.buf[lax.rem(self.y - j + NY, NY)]

    def scatter(self):
        self.out_copies = started([
            send(self.src.at[lax.rem(self.y + k, NY)], self.buf.at[k], self.out_sems, k, self.at_y(k))
            for k in range(1, NY)
        ])
        self.buf[0] = self.src[self.y]

    def group_copy(self, far):
        there = (self.dp, (self.z + self.step * far) * NY + self.y)
        return send(self.total, self.group.at[far - 1], self.group_sems, far - 1, there)

    def has(self, far):
        other = self.z + far
        return (other >= 0) & (other < NZL)

    def totals(self):
        for copy in self.out_copies:
            copy.wait_recv()
        total = jnp.zeros((WIDTH, WIDTH), f32)
        for j in self.order:
            total = self.carry(j) * total + self.block(j)
        self.total[...] = total
        for far in (1, 2):
            pl.when(self.has(self.step * far))(lambda far=far: self.group_copy(far).start())

    def give_back(self):
        for far in (1, 2):
            source = self.has(-self.step * far)
            pl.when(source)(lambda far=far: self.group_copy(far).wait_recv())

            @pl.when(jnp.logical_not(source))
            def _():
                self.group[far - 1] = jnp.zeros((WIDTH, WIDTH), f32)

        now = self.group[0] + self.carry(8 if self.step > 0 else 9) * self.group[1]
        for j in self.order:
            self.back[j] = now
            now = self.carry(j) * now + self.block(j)
        self.back_copies = started([
            send(self.back.at[lax.rem(self.y + k, NY)], self.result.at[self.y], self.back_sems, k, self.at_y(k))
            for k in range(1, NY)
        ])
        self.result[self.y] = self.back[self.y]

    def finish(self):
        for k in range(1, NY):
            send(
                self.back.at[0], self.result.at[lax.rem(self.y - k + NY, NY)],
                self.back_sems, k, self.at_y(k),
            ).wait_recv()
        for far in (1, 2):
            pl.when(self.has(self.step * far))(lambda far=far: self.group_copy(far).wait_send())
        for copy in self.out_copies + self.back_copies:
            copy.wait_send()


HEADS_BUF = pltpu.VMEM((HEADS, WIDTH, WIDTH), f32)
SCAN_BUFS = [HEADS_BUF, HEADS_BUF, pltpu.VMEM((WIDTH, WIDTH), f32), pltpu.VMEM((2, WIDTH, WIDTH), f32)]
SCAN_SEMS = [pltpu.SemaphoreType.DMA((NY,))] * 4 + [pltpu.SemaphoreType.DMA((2,))] * 2


def greet(devices):
    barrier = pltpu.get_barrier_semaphore()
    for device in devices:
        pl.semaphore_signal(barrier, inc=1, device_id=device, device_id_type=MESH)
    pl.semaphore_wait(barrier, len(devices))


def scan_kernel(state_ref, carry_ref, in_ref, *scratch):
    dp, ctx, z, y = place()
    scan = Scan(1, state_ref, carry_ref, in_ref, scratch[:4], scratch[4:6], scratch[6:8], scratch[8:10])
    greet(
        [scan.at_y(k) for k in range(1, NY)]
        + [(dp, lax.rem(z + k, NZL) * NY + y) for k in range(1, NZL)]
    )
    scan.scatter()
    scan.totals()
    scan.give_back()
    scan.finish()


def attention_kernel(
    q_ref, k_ref, v_ref, layer_ref, gain_ref, rate_ref, len_ref, in_ref,
    px_ref, pz_ref, attention_buf, normed_buf,
):
    base = lax.axis_index("ctx") * ROWS
    bounds = doc_bounds(len_ref)
    offsets, entering, _ = edge_tables(base, bounds)
    same, distance = pair_tables(base, bounds)
    for h in range(HEADS):
        cols = pl.ds(h * WIDTH, WIDTH)
        rate = rate_ref[h]
        q, k, v = q_ref[:, cols], k_ref[:, cols], v_ref[:, cols]
        mask = jnp.where(same, jnp.exp(-rate * distance), 0.0)
        entry = jnp.where(entering, jnp.exp(-rate * offsets), 0.0)
        s_high, s_low = split(matmul(q, k, NT) * mask)
        in_high, in_low = split(in_ref[h])
        attention = matmul(s_high, v, NN) + matmul(s_low, v, NN)
        attention += entry * (matmul(q, in_high, NN) + matmul(q, in_low, NN))
        attention_buf[:, cols] = attention
    attention = attention_buf[...]
    mean = jnp.mean(attention * attention, axis=-1, keepdims=True)
    normed_buf[...] = (attention * lax.rsqrt(mean + norm_eps) * gain_ref[...]).astype(bf16)
    for h in range(HEADS):
        x, z_high = h // 2, h % 2
        product = matmul(normed_buf[:, pl.ds(h * WIDTH, WIDTH)], layer_ref[...], TN)
        for core in range(2):
            px_ref[x, z_high, core] = product[core * 64:core * 64 + 64, :XCOLS]
            for z_low in range(NZL):
                row = core * 64 + z_low * 16
                pz_ref[z_high * 4 + z_low, core, x] = product[row:row + 16, XCOLS:]


def pair_tables(base, bounds):
    rows = lax.broadcasted_iota(jnp.int32, (ROWS, ROWS), 0)
    columns = lax.broadcasted_iota(jnp.int32, (ROWS, ROWS), 1)
    same = (doc_of(base + rows, bounds) == doc_of(base + columns, bounds)) & (rows >= columns)
    return same, jnp.maximum(rows - columns, 0).astype(f32)


def gradients_kernel(
    q_ref, k_ref, v_ref, g_ref, rate_ref, len_ref, in_ref, grad_ref, dq_ref, dk_ref, dv_ref,
):
    base = lax.axis_index("ctx") * ROWS
    bounds = doc_bounds(len_ref)
    offsets, entering, leaving = edge_tables(base, bounds)
    same, distance = pair_tables(base, bounds)
    for h in range(HEADS):
        cols = pl.ds(h * WIDTH, WIDTH)
        rate = rate_ref[h]
        q, k, v, g = q_ref[:, cols], k_ref[:, cols], v_ref[:, cols], g_ref[:, cols]
        mask = jnp.where(same, jnp.exp(-rate * distance), 0.0)
        entry = jnp.where(entering, jnp.exp(-rate * offsets), 0.0)
        leave = jnp.where(leaving, jnp.exp(-rate * (ROWS - offsets)), 0.0)
        s_high, s_low = split(matmul(q, k, NT) * mask)
        d_high, d_low = split(matmul(g, v, NT) * mask)
        in_high, in_low = split(in_ref[h])
        grad_high, grad_low = split(grad_ref[h])
        dq = matmul(d_high, k, NN) + matmul(d_low, k, NN)
        dq += entry * (matmul(g, in_high, NT) + matmul(g, in_low, NT))
        dq_ref[:, cols] = dq.astype(bf16)
        dk = matmul(d_high, q, TN) + matmul(d_low, q, TN)
        dk += leave * (matmul(v, grad_high, NT) + matmul(v, grad_low, NT))
        dk_ref[:, cols] = dk.astype(bf16)
        dv = matmul(s_high, g, TN) + matmul(s_low, g, TN)
        dv += leave * (matmul(k, grad_high, NN) + matmul(k, grad_low, NN))
        dv_ref[:, cols] = dv.astype(bf16)


def reduce_kernel(
    scale, px_ref, pz_ref, pull_ref, carry_ref, out_ref, grad_ref,
    cx_buf, ax_buf, x_buf, bx_buf, xz_buf, cz_buf, az_buf, z_buf, bz_buf, zx_buf, c_buf, y_buf,
    core_send, core_recv, x_send, x_recv, xz_send, xz_recv,
    z_send, z_recv, zx_send, zx_recv, y_send, y_recv, *scratch,
):
    dp, ctx, z_low, y = place()
    x, z_high, core = dp // 4, lax.rem(dp // 2, 2), lax.rem(dp, 2)
    z = z_high * 4 + z_low
    twin = (dp + 1 - 2 * core, ctx)

    def at_x(k):
        return (lax.rem(x + k, NX) * 4 + lax.rem(dp, 4), ctx)

    def at_z(k):
        there = lax.rem(z + k, NZ)
        return (x * 4 + there // 4 * 2 + core, lax.rem(there, 4) * NY + y)

    def at_y(k):
        return (dp, ctx - y + lax.rem(y + k, NY))

    scan = Scan(-1, pull_ref, carry_ref, grad_ref, scratch[:4], scratch[4:6], scratch[6:8], scratch[8:10])
    greet(
        [twin] + [at_x(k) for k in range(1, NX)] + [at_z(k) for k in range(1, NZ)]
        + [at_y(k) for k in range(1, NY)]
    )
    core_sems = (core_send, core_recv)
    order = tuple(range(1, NX)) + (0,)
    core_copies = started(
        [send(pz_ref.at[:, 1 - core], cz_buf, core_sems, NX, twin)]
        + [
            send(px_ref.at[lax.rem(x + k, NX), :, 1 - core], cx_buf.at[k], core_sems, k, twin)
            for k in order
        ]
    )
    scan.scatter()
    core_copies[0].wait_recv()
    az_buf[...] = pz_ref[:, core] + cz_buf[...]
    z_copies = started([
        send(az_buf.at[lax.rem(z + k, NZ)], z_buf.at[k], (z_send, z_recv), k, at_z(k))
        for k in range(1, NZ)
    ])
    x_copies = []
    for k, copy in zip(order, core_copies[1:]):
        copy.wait_recv()
        ax_buf[k] = px_ref[lax.rem(x + k, NX), :, core] + cx_buf[k]
        if k:
            x_copies += started([send(ax_buf.at[k], x_buf.at[k], (x_send, x_recv), k, at_x(k))])

    def gather(total, copies, buf):
        for k, copy in enumerate(copies, 1):
            copy.wait_recv()
            total = total + buf[k]
        return total

    bx_buf[...] = gather(ax_buf[0], x_copies, x_buf).reshape(bx_buf.shape)
    xz_copies = started([
        send(bx_buf.at[lax.rem(z + k, NZ)], xz_buf.at[k], (xz_send, xz_recv), k, at_z(k))
        for k in range(1, NZ)
    ])
    bz_buf[...] = gather(az_buf[z], z_copies, z_buf)
    zx_copies = started([
        send(bz_buf.at[lax.rem(x + k, NX)], zx_buf.at[k], (zx_send, zx_recv), k, at_x(k))
        for k in range(1, NX)
    ])
    scan.totals()
    scan.give_back()
    right = gather(bz_buf[x], zx_copies, zx_buf)
    left = gather(bx_buf[z], xz_copies, xz_buf)
    for j in range(NY):
        c_buf[j, :, :XCOLS] = left[2 * j:2 * j + 2, :]
        c_buf[j, :, XCOLS:] = right[2 * j:2 * j + 2, :]
    y_copies = started([
        send(c_buf.at[lax.rem(y + k, NY)], y_buf.at[k], (y_send, y_recv), k, at_y(k))
        for k in range(1, NY)
    ])
    out_ref[...] = gather(c_buf[y], y_copies, y_buf) * scale
    scan.finish()
    for copy in core_copies + x_copies + z_copies + xz_copies + zx_copies + y_copies:
        copy.wait_send()


def on_device(queries, keys, values, out_grad, layer_grad, norm_gain, decay_rates, doc_lengths):
    rows, features, bucket = ROWS, HEADS * WIDTH, layer_grad.shape[2]
    scale = 1.0 / math.sqrt(rows * lax.axis_size("dp") * lax.axis_size("ctx"))
    q, k, v, g = (a.reshape(rows, features) for a in (queries, keys, values, out_grad))
    layer = layer_grad.reshape(rows, bucket)
    states = jax.ShapeDtypeStruct((HEADS, WIDTH, WIDTH), f32)
    state, pull, carry = pl.pallas_call(
        summary_kernel,
        out_shape=(states, states, jax.ShapeDtypeStruct((16, WIDTH), f32)),
        in_specs=[VMEM_SPEC] * 4 + [SMEM_SPEC] * 2,
        out_specs=(VMEM_SPEC,) * 3,
        name="summary",
    )(q, k, v, g, decay_rates, doc_lengths)
    state_in = pl.pallas_call(
        scan_kernel,
        out_shape=states,
        in_specs=[VMEM_SPEC] * 2,
        out_specs=VMEM_SPEC,
        scratch_shapes=SCAN_BUFS + SCAN_SEMS,
        compiler_params=pltpu.CompilerParams(collective_id=0, has_side_effects=True),
        name="scan",
    )(state, carry)
    zcols = bucket - XCOLS
    product_shapes = (
        jax.ShapeDtypeStruct((NX, 2, 2, 64, XCOLS), f32),
        jax.ShapeDtypeStruct((NZ, 2, NX, 16, zcols), f32),
    )
    px, pz = pl.pallas_call(
        attention_kernel,
        out_shape=product_shapes,
        in_specs=[VMEM_SPEC] * 5 + [SMEM_SPEC] * 2 + [VMEM_SPEC],
        out_specs=(VMEM_SPEC,) * 2,
        scratch_shapes=[pltpu.VMEM((rows, features), f32), pltpu.VMEM((rows, features), bf16)],
        name="attention",
    )(q, k, v, layer, norm_gain.reshape(1, features), decay_rates, doc_lengths, state_in)
    dma = pltpu.SemaphoreType.DMA
    proj_grad, state_grad = pl.pallas_call(
        functools.partial(reduce_kernel, scale),
        out_shape=(jax.ShapeDtypeStruct((2, bucket), f32), states),
        in_specs=[VMEM_SPEC] * 4,
        out_specs=(VMEM_SPEC,) * 2,
        scratch_shapes=[pltpu.VMEM((NX, 2, 64, XCOLS), f32)] * 3
        + [pltpu.VMEM((NZ, 16, XCOLS), f32)] * 2
        + [pltpu.VMEM((NZ, NX, 16, zcols), f32)] * 3
        + [pltpu.VMEM((NX, 16, zcols), f32)] * 2
        + [pltpu.VMEM((NY, 2, bucket), f32)] * 2
        + [dma((NX + 1,))] * 2 + [dma((NX,))] * 2 + [dma((NZ,))] * 4
        + [dma((NX,))] * 2 + [dma((NY,))] * 2
        + SCAN_BUFS + SCAN_SEMS,
        compiler_params=pltpu.CompilerParams(collective_id=1, has_side_effects=True),
        name="reduce",
    )(px, pz, pull, carry)
    grad_shape = jax.ShapeDtypeStruct((rows, features), bf16)
    query_grad, key_grad, value_grad = pl.pallas_call(
        gradients_kernel,
        out_shape=(grad_shape,) * 3,
        in_specs=[VMEM_SPEC] * 4 + [SMEM_SPEC] * 2 + [VMEM_SPEC] * 2,
        out_specs=(VMEM_SPEC,) * 3,
        name="gradients",
    )(q, k, v, g, decay_rates, doc_lengths, state_in, state_grad)
    shape_out = (1, rows, features)
    return (
        query_grad.reshape(shape_out),
        key_grad.reshape(shape_out),
        value_grad.reshape(shape_out),
        proj_grad,
    )


def solution(mesh):
    block = P("dp", "ctx", None)
    return jax.shard_map(
        on_device,
        mesh=mesh,
        in_specs=(block,) * 5 + (P(), P(), P("dp", None)),
        out_specs=(block,) * 3 + (P(("dp", "ctx"), None),),
        check_vma=False,
    )
```

```python
import functools
import math

import jax
import jax.numpy as jnp
from jax import lax
from jax.experimental import pallas as pl
from jax.experimental.pallas import tpu as pltpu
from jax.sharding import PartitionSpec as P

norm_eps = 1e-06
HEADS, WIDTH, ROWS = 8, 128, 128
NX, NZ, NY, NZL = 4, 8, 8, 4
XCOLS = 512
MESH = pl.DeviceIdType.MESH
f32, bf16 = jnp.float32, jnp.bfloat16
VMEM_SPEC = pl.BlockSpec(memory_space=pltpu.VMEM)
SMEM_SPEC = pl.BlockSpec(memory_space=pltpu.SMEM)


def split(value):
    high = value.astype(bf16)
    return high, (value - high.astype(f32)).astype(bf16)


def matmul(a, b, dims):
    return lax.dot_general(a, b, (dims, ((), ())), preferred_element_type=f32)


NN, NT, TN = ((1,), (0,)), ((1,), (1,)), ((0,), (0,))


def doc_bounds(len_ref):
    first = len_ref[0, 0]
    second = first + len_ref[0, 1]
    return first, second, second + len_ref[0, 2]


def doc_of(positions, bounds):
    return sum((positions >= bound).astype(jnp.int32) for bound in bounds)


def doc_of_scalar(position, bounds):
    return sum(jnp.where(position >= bound, 1, 0) for bound in bounds)


def edge_tables(base, bounds):
    offsets = lax.broadcasted_iota(jnp.int32, (ROWS, WIDTH), 0)
    docs = doc_of(base + offsets, bounds)
    entering = docs == doc_of_scalar(base - 1, bounds)
    leaving = docs == doc_of_scalar(base + ROWS - 1, bounds)
    return offsets.astype(f32), entering, leaving


def summary_kernel(q_ref, k_ref, v_ref, g_ref, rate_ref, len_ref, state_ref, pull_ref, carry_ref):
    ctx = lax.axis_index("ctx")
    bounds = doc_bounds(len_ref)
    offsets, entering, leaving = edge_tables(ctx * ROWS, bounds)
    for h in range(HEADS):
        cols = pl.ds(h * WIDTH, WIDTH)
        rate = rate_ref[h]
        entry = jnp.where(entering, jnp.exp(-rate * offsets), 0.0)
        leave = jnp.where(leaving, jnp.exp(-rate * (ROWS - offsets)), 0.0)
        high, low = split(k_ref[:, cols].astype(f32) * leave)
        v = v_ref[:, cols]
        state_ref[h] = matmul(high, v, TN) + matmul(low, v, TN)
        high, low = split(q_ref[:, cols].astype(f32) * entry)
        g = g_ref[:, cols]
        pull_ref[h] = matmul(high, g, TN) + matmul(low, g, TN)
    group, own = ctx // NY, lax.rem(ctx, NY)
    rate = rate_ref[own]

    def carry(first, blocks):
        start = first * ROWS
        whole = doc_of_scalar(start - 1, bounds) == doc_of_scalar(start + blocks * ROWS - 1, bounds)
        decay = jnp.exp(jnp.full((1, WIDTH), -rate * float(blocks * ROWS), f32))
        return jnp.where(whole, decay, 0.0)

    for j in range(NY):
        carry_ref[pl.ds(j, 1), :] = carry(group * NY + j, 1)
    carry_ref[pl.ds(8, 1), :] = carry((group - 1) * NY, NY)
    carry_ref[pl.ds(9, 1), :] = carry((group + 1) * NY, NY)


def place():
    dp, ctx = lax.axis_index("dp"), lax.axis_index("ctx")
    return dp, ctx, ctx // NY, lax.rem(ctx, NY)


def send(src, dst, sems, at, device):
    return pltpu.make_async_remote_copy(
        src_ref=src, dst_ref=dst, send_sem=sems[0].at[at], recv_sem=sems[1].at[at],
        device_id=device, device_id_type=MESH,
    )


def started(copies):
    for copy in copies:
        copy.start()
    return copies


class Scan:
    def __init__(self, step, src, carry, result, bufs, out_sems, back_sems, group_sems):
        self.step, self.src, self.carry_ref, self.result = step, src, carry, result
        self.buf, self.back, self.total, self.group = bufs
        self.out_sems, self.back_sems, self.group_sems = out_sems, back_sems, group_sems
        self.dp, _, self.z, self.y = place()
        self.out_copies = []
        self.order = range(NY) if step > 0 else range(NY - 1, -1, -1)

    def at_y(self, k):
        return (self.dp, self.z * NY + lax.rem(self.y + k, NY))

    def carry(self, j):
        return self.carry_ref[pl.ds(j, 1), :]

    def block(self, j):
        return self.buf[lax.rem(self.y - j + NY, NY)]

    def scatter(self, offsets):
        self.out_copies += started([
            send(self.src.at[lax.rem(self.y + k, NY)], self.buf.at[k], self.out_sems, k, self.at_y(k))
            for k in offsets
        ])

    def group_copy(self, far):
        there = (self.dp, (self.z + self.step * far) * NY + self.y)
        return send(self.total, self.group.at[far - 1], self.group_sems, far - 1, there)

    def has(self, far):
        other = self.z + far
        return (other >= 0) & (other < NZL)

    def totals(self):
        self.buf[0] = self.src[self.y]
        for copy in self.out_copies:
            copy.wait_recv()
        total = jnp.zeros((WIDTH, WIDTH), f32)
        for j in self.order:
            total = self.carry(j) * total + self.block(j)
        self.total[...] = total
        for far in (1, 2):
            pl.when(self.has(self.step * far))(lambda far=far: self.group_copy(far).start())

    def give_back(self):
        for far in (1, 2):
            source = self.has(-self.step * far)
            pl.when(source)(lambda far=far: self.group_copy(far).wait_recv())

            @pl.when(jnp.logical_not(source))
            def _():
                self.group[far - 1] = jnp.zeros((WIDTH, WIDTH), f32)

        now = self.group[0] + self.carry(8 if self.step > 0 else 9) * self.group[1]
        for j in self.order:
            self.back[j] = now
            now = self.carry(j) * now + self.block(j)
        self.back_copies = started([
            send(self.back.at[lax.rem(self.y + k, NY)], self.result.at[self.y], self.back_sems, k, self.at_y(k))
            for k in range(1, NY)
        ])
        self.result[self.y] = self.back[self.y]

    def arrive(self):
        for k in range(1, NY):
            send(
                self.back.at[0], self.result.at[lax.rem(self.y - k + NY, NY)],
                self.back_sems, k, self.at_y(k),
            ).wait_recv()

    def finish(self):
        for far in (1, 2):
            pl.when(self.has(self.step * far))(lambda far=far: self.group_copy(far).wait_send())
        for copy in self.out_copies + self.back_copies:
            copy.wait_send()


HEADS_BUF = pltpu.VMEM((HEADS, WIDTH, WIDTH), f32)
SCAN_BUFS = [HEADS_BUF, HEADS_BUF, pltpu.VMEM((WIDTH, WIDTH), f32), pltpu.VMEM((2, WIDTH, WIDTH), f32)]
SCAN_SEMS = [pltpu.SemaphoreType.DMA((NY,))] * 4 + [pltpu.SemaphoreType.DMA((2,))] * 2


def greet(devices):
    barrier = pltpu.get_barrier_semaphore()
    for device in devices:
        pl.semaphore_signal(barrier, inc=1, device_id=device, device_id_type=MESH)
    pl.semaphore_wait(barrier, len(devices))


def attention_part(
    q_ref, k_ref, v_ref, layer_ref, gain_ref, rate_ref, len_ref, in_ref,
    px_ref, pz_ref, attention_buf, normed_buf,
):
    base = lax.axis_index("ctx") * ROWS
    bounds = doc_bounds(len_ref)
    offsets, entering, _ = edge_tables(base, bounds)
    same, distance = pair_tables(base, bounds)
    for h in range(HEADS):
        cols = pl.ds(h * WIDTH, WIDTH)
        rate = rate_ref[h]
        q, k, v = q_ref[:, cols], k_ref[:, cols], v_ref[:, cols]
        mask = jnp.where(same, jnp.exp(-rate * distance), 0.0)
        entry = jnp.where(entering, jnp.exp(-rate * offsets), 0.0)
        s_high, s_low = split(matmul(q, k, NT) * mask)
        in_high, in_low = split(in_ref[h])
        attention = matmul(s_high, v, NN) + matmul(s_low, v, NN)
        attention += entry * (matmul(q, in_high, NN) + matmul(q, in_low, NN))
        attention_buf[:, cols] = attention
    attention = attention_buf[...]
    mean = jnp.mean(attention * attention, axis=-1, keepdims=True)
    normed_buf[...] = (attention * lax.rsqrt(mean + norm_eps) * gain_ref[...]).astype(bf16)
    for h in range(HEADS):
        x, z_high = h // 2, h % 2
        product = matmul(normed_buf[:, pl.ds(h * WIDTH, WIDTH)], layer_ref[...], TN)
        for core in range(2):
            px_ref[x, z_high, core] = product[core * 64:core * 64 + 64, :XCOLS]
            for z_low in range(NZL):
                row = core * 64 + z_low * 16
                pz_ref[z_high * 4 + z_low, core, x] = product[row:row + 16, XCOLS:]


def pair_tables(base, bounds):
    rows = lax.broadcasted_iota(jnp.int32, (ROWS, ROWS), 0)
    columns = lax.broadcasted_iota(jnp.int32, (ROWS, ROWS), 1)
    same = (doc_of(base + rows, bounds) == doc_of(base + columns, bounds)) & (rows >= columns)
    return same, jnp.maximum(rows - columns, 0).astype(f32)


def block_part(q_ref, k_ref, v_ref, g_ref, rate_ref, len_ref, in_ref, dq_ref, dk_ref, dv_ref):
    base = lax.axis_index("ctx") * ROWS
    bounds = doc_bounds(len_ref)
    offsets, entering, _ = edge_tables(base, bounds)
    same, distance = pair_tables(base, bounds)
    for h in range(HEADS):
        cols = pl.ds(h * WIDTH, WIDTH)
        rate = rate_ref[h]
        q, k, v, g = q_ref[:, cols], k_ref[:, cols], v_ref[:, cols], g_ref[:, cols]
        mask = jnp.where(same, jnp.exp(-rate * distance), 0.0)
        entry = jnp.where(entering, jnp.exp(-rate * offsets), 0.0)
        s_high, s_low = split(matmul(q, k, NT) * mask)
        d_high, d_low = split(matmul(g, v, NT) * mask)
        in_high, in_low = split(in_ref[h])
        dq = matmul(d_high, k, NN) + matmul(d_low, k, NN)
        dq += entry * (matmul(g, in_high, NT) + matmul(g, in_low, NT))
        dq_ref[:, cols] = dq.astype(bf16)
        dk_ref[:, cols] = matmul(d_high, q, TN) + matmul(d_low, q, TN)
        dv_ref[:, cols] = matmul(s_high, g, TN) + matmul(s_low, g, TN)


def gradients_kernel(
    k_ref, v_ref, rate_ref, len_ref, grad_ref, dq_part, dk_part, dv_part, dq_ref, dk_ref, dv_ref,
):
    offsets, _, leaving = edge_tables(lax.axis_index("ctx") * ROWS, doc_bounds(len_ref))
    dq_ref[...] = dq_part[...]
    for h in range(HEADS):
        cols = pl.ds(h * WIDTH, WIDTH)
        k, v = k_ref[:, cols], v_ref[:, cols]
        leave = jnp.where(leaving, jnp.exp(-rate_ref[h] * (ROWS - offsets)), 0.0)
        grad_high, grad_low = split(grad_ref[h])
        dk = leave * (matmul(v, grad_high, NT) + matmul(v, grad_low, NT))
        dk_ref[:, cols] = (dk_part[:, cols] + dk).astype(bf16)
        dv = leave * (matmul(k, grad_high, NN) + matmul(k, grad_low, NN))
        dv_ref[:, cols] = (dv_part[:, cols] + dv).astype(bf16)


def main_kernel(
    scale, q_ref, k_ref, v_ref, g_ref, layer_ref, gain_ref, rate_ref, len_ref,
    state_ref, pull_ref, carry_ref,
    out_ref, grad_ref, dq_ref, dk_ref, dv_ref,
    in_ref, px_ref, pz_ref, attention_buf, normed_buf, cx_buf, ax_buf, x_buf, bx_buf, xz_buf, cz_buf, az_buf, z_buf, bz_buf, zx_buf, c_buf, y_buf,
    core_send, core_recv, x_send, x_recv, xz_send, xz_recv,
    z_send, z_recv, zx_send, zx_recv, y_send, y_recv, *scratch,
):
    dp, ctx, z_low, y = place()
    x, z_high, core = dp // 4, lax.rem(dp // 2, 2), lax.rem(dp, 2)
    z = z_high * 4 + z_low
    twin = (dp + 1 - 2 * core, ctx)

    def at_x(k):
        return (lax.rem(x + k, NX) * 4 + lax.rem(dp, 4), ctx)

    def at_z(k):
        there = lax.rem(z + k, NZ)
        return (x * 4 + there // 4 * 2 + core, lax.rem(there, 4) * NY + y)

    def at_y(k):
        return (dp, ctx - y + lax.rem(y + k, NY))

    def scan_of(step, src, result, own):
        return Scan(step, src, carry_ref, result, own[:4], own[4:6], own[6:8], own[8:10])

    ahead = scan_of(1, state_ref, in_ref, scratch[:10])
    scan = scan_of(-1, pull_ref, grad_ref, scratch[10:])
    greet(
        [twin] + [at_x(k) for k in range(1, NX)] + [at_z(k) for k in range(1, NZ)]
        + [at_y(k) for k in range(1, NY)]
    )
    ahead.scatter(range(1, NY))
    ahead.totals()
    scan.scatter((1, 7, 2, 6))
    ahead.give_back()
    scan.scatter((3, 5, 4))
    ahead.arrive()
    attention_part(
        q_ref, k_ref, v_ref, layer_ref, gain_ref, rate_ref, len_ref, in_ref,
        px_ref, pz_ref, attention_buf, normed_buf,
    )
    core_sems = (core_send, core_recv)
    order = tuple(range(1, NX)) + (0,)
    core_copies = started(
        [send(pz_ref.at[:, 1 - core], cz_buf, core_sems, NX, twin)]
        + [
            send(px_ref.at[lax.rem(x + k, NX), :, 1 - core], cx_buf.at[k], core_sems, k, twin)
            for k in order
        ]
    )
    core_copies[0].wait_recv()
    az_buf[...] = pz_ref[:, core] + cz_buf[...]
    z_copies = started([
        send(az_buf.at[lax.rem(z + k, NZ)], z_buf.at[k], (z_send, z_recv), k, at_z(k))
        for k in range(1, NZ)
    ])
    x_copies = []
    for k, copy in zip(order, core_copies[1:]):
        copy.wait_recv()
        ax_buf[k] = px_ref[lax.rem(x + k, NX), :, core] + cx_buf[k]
        if k:
            x_copies += started([send(ax_buf.at[k], x_buf.at[k], (x_send, x_recv), k, at_x(k))])

    block_part(q_ref, k_ref, v_ref, g_ref, rate_ref, len_ref, in_ref, dq_ref, dk_ref, dv_ref)
    scan.totals()

    def gather(total, copies, buf):
        for k, copy in enumerate(copies, 1):
            copy.wait_recv()
            total = total + buf[k]
        return total

    bx_buf[...] = gather(ax_buf[0], x_copies, x_buf).reshape(bx_buf.shape)
    xz_copies = started([
        send(bx_buf.at[lax.rem(z + k, NZ)], xz_buf.at[k], (xz_send, xz_recv), k, at_z(k))
        for k in range(1, NZ)
    ])
    scan.give_back()
    bz_buf[...] = gather(az_buf[z], z_copies, z_buf)
    zx_copies = started([
        send(bz_buf.at[lax.rem(x + k, NX)], zx_buf.at[k], (zx_send, zx_recv), k, at_x(k))
        for k in range(1, NX)
    ])
    right = gather(bz_buf[x], zx_copies, zx_buf)
    left = gather(bx_buf[z], xz_copies, xz_buf)
    for j in range(NY):
        c_buf[j, :, :XCOLS] = left[2 * j:2 * j + 2, :]
        c_buf[j, :, XCOLS:] = right[2 * j:2 * j + 2, :]
    y_copies = started([
        send(c_buf.at[lax.rem(y + k, NY)], y_buf.at[k], (y_send, y_recv), k, at_y(k))
        for k in range(1, NY)
    ])
    out_ref[...] = gather(c_buf[y], y_copies, y_buf) * scale
    scan.arrive()
    scan.finish()
    ahead.finish()
    for copy in core_copies + x_copies + z_copies + xz_copies + zx_copies + y_copies:
        copy.wait_send()


def on_device(queries, keys, values, out_grad, layer_grad, norm_gain, decay_rates, doc_lengths):
    rows, features, bucket = ROWS, HEADS * WIDTH, layer_grad.shape[2]
    scale = 1.0 / math.sqrt(rows * lax.axis_size("dp") * lax.axis_size("ctx"))
    q, k, v, g = (a.reshape(rows, features) for a in (queries, keys, values, out_grad))
    layer = layer_grad.reshape(rows, bucket)
    states = jax.ShapeDtypeStruct((HEADS, WIDTH, WIDTH), f32)
    state, pull, carry = pl.pallas_call(
        summary_kernel,
        out_shape=(states, states, jax.ShapeDtypeStruct((16, WIDTH), f32)),
        in_specs=[VMEM_SPEC] * 4 + [SMEM_SPEC] * 2,
        out_specs=(VMEM_SPEC,) * 3,
        name="summary",
    )(q, k, v, g, decay_rates, doc_lengths)
    zcols = bucket - XCOLS
    dma = pltpu.SemaphoreType.DMA
    part = jax.ShapeDtypeStruct((rows, features), f32)
    grad_shape = jax.ShapeDtypeStruct((rows, features), bf16)
    proj_grad, state_grad, *parts = pl.pallas_call(
        functools.partial(main_kernel, scale),
        out_shape=(jax.ShapeDtypeStruct((2, bucket), f32), states, grad_shape, part, part),
        in_specs=[VMEM_SPEC] * 6 + [SMEM_SPEC] * 2 + [VMEM_SPEC] * 3,
        out_specs=(VMEM_SPEC,) * 5,
        scratch_shapes=[
            HEADS_BUF,
            pltpu.VMEM((NX, 2, 2, 64, XCOLS), f32),
            pltpu.VMEM((NZ, 2, NX, 16, zcols), f32),
            pltpu.VMEM((rows, features), f32),
            pltpu.VMEM((rows, features), bf16),
        ]
        + [pltpu.VMEM((NX, 2, 64, XCOLS), f32)] * 3
        + [pltpu.VMEM((NZ, 16, XCOLS), f32)] * 2
        + [pltpu.VMEM((NZ, NX, 16, zcols), f32)] * 3
        + [pltpu.VMEM((NX, 16, zcols), f32)] * 2
        + [pltpu.VMEM((NY, 2, bucket), f32)] * 2
        + [dma((NX + 1,))] * 2 + [dma((NX,))] * 2 + [dma((NZ,))] * 4
        + [dma((NX,))] * 2 + [dma((NY,))] * 2
        + (SCAN_BUFS + SCAN_SEMS) * 2,
        compiler_params=pltpu.CompilerParams(collective_id=0, has_side_effects=True),
        name="main",
    )(q, k, v, g, layer, norm_gain.reshape(1, features), decay_rates, doc_lengths, state, pull, carry)
    query_grad, key_grad, value_grad = pl.pallas_call(
        gradients_kernel,
        out_shape=(grad_shape,) * 3,
        in_specs=[VMEM_SPEC] * 2 + [SMEM_SPEC] * 2 + [VMEM_SPEC] * 4,
        out_specs=(VMEM_SPEC,) * 3,
        name="gradients",
    )(k, v, decay_rates, doc_lengths, state_grad, *parts)
    shape_out = (1, rows, features)
    return (
        query_grad.reshape(shape_out),
        key_grad.reshape(shape_out),
        value_grad.reshape(shape_out),
        proj_grad,
    )


def solution(mesh):
    block = P("dp", "ctx", None)
    return jax.shard_map(
        on_device,
        mesh=mesh,
        in_specs=(block,) * 5 + (P(), P(), P("dp", None)),
        out_specs=(block,) * 3 + (P(("dp", "ctx"), None),),
        check_vma=False,
    )
```

```python
import functools
import math

import jax
import jax.numpy as jnp
from jax import lax
from jax.experimental import pallas as pl
from jax.experimental.pallas import tpu as pltpu
from jax.sharding import PartitionSpec as P

norm_eps = 1e-06
HEADS, WIDTH, ROWS = 8, 128, 128
NX, NZ, NY, NZL = 4, 8, 8, 4
XCOLS = 512
MESH = pl.DeviceIdType.MESH
f32, bf16 = jnp.float32, jnp.bfloat16
VMEM_SPEC = pl.BlockSpec(memory_space=pltpu.VMEM)
SMEM_SPEC = pl.BlockSpec(memory_space=pltpu.SMEM)


def split(value):
    high = value.astype(bf16)
    return high, (value - high.astype(f32)).astype(bf16)


def matmul(a, b, dims):
    return lax.dot_general(a, b, (dims, ((), ())), preferred_element_type=f32)


NN, NT, TN = ((1,), (0,)), ((1,), (1,)), ((0,), (0,))


def doc_bounds(len_ref):
    first = len_ref[0, 0]
    second = first + len_ref[0, 1]
    return first, second, second + len_ref[0, 2]


def doc_of(positions, bounds):
    return sum((positions >= bound).astype(jnp.int32) for bound in bounds)


def doc_of_scalar(position, bounds):
    return sum(jnp.where(position >= bound, 1, 0) for bound in bounds)


def edge_tables(base, bounds):
    offsets = lax.broadcasted_iota(jnp.int32, (ROWS, WIDTH), 0)
    docs = doc_of(base + offsets, bounds)
    entering = docs == doc_of_scalar(base - 1, bounds)
    leaving = docs == doc_of_scalar(base + ROWS - 1, bounds)
    return offsets.astype(f32), entering, leaving


def state_part(k_ref, v_ref, rate_ref, len_ref, state_ref, carry_ref):
    ctx = lax.axis_index("ctx")
    bounds = doc_bounds(len_ref)
    offsets, _, leaving = edge_tables(ctx * ROWS, bounds)
    for h in range(HEADS):
        cols = pl.ds(h * WIDTH, WIDTH)
        leave = jnp.where(leaving, jnp.exp(-rate_ref[h] * (ROWS - offsets)), 0.0)
        high, low = split(k_ref[:, cols].astype(f32) * leave)
        v = v_ref[:, cols]
        state_ref[h] = matmul(high, v, TN) + matmul(low, v, TN)
    group, own = ctx // NY, lax.rem(ctx, NY)
    rate = rate_ref[own]

    def carry(first, blocks):
        start = first * ROWS
        whole = doc_of_scalar(start - 1, bounds) == doc_of_scalar(start + blocks * ROWS - 1, bounds)
        decay = jnp.exp(jnp.full((1, WIDTH), -rate * float(blocks * ROWS), f32))
        return jnp.where(whole, decay, 0.0)

    for j in range(NY):
        carry_ref[pl.ds(j, 1), :] = carry(group * NY + j, 1)
    carry_ref[pl.ds(8, 1), :] = carry((group - 1) * NY, NY)
    carry_ref[pl.ds(9, 1), :] = carry((group + 1) * NY, NY)


def pull_part(q_ref, g_ref, rate_ref, len_ref, pull_ref):
    offsets, entering, _ = edge_tables(lax.axis_index("ctx") * ROWS, doc_bounds(len_ref))
    for h in range(HEADS):
        cols = pl.ds(h * WIDTH, WIDTH)
        entry = jnp.where(entering, jnp.exp(-rate_ref[h] * offsets), 0.0)
        high, low = split(q_ref[:, cols].astype(f32) * entry)
        g = g_ref[:, cols]
        pull_ref[h] = matmul(high, g, TN) + matmul(low, g, TN)


def place():
    dp, ctx = lax.axis_index("dp"), lax.axis_index("ctx")
    return dp, ctx, ctx // NY, lax.rem(ctx, NY)


def send(src, dst, sems, at, device):
    return pltpu.make_async_remote_copy(
        src_ref=src, dst_ref=dst, send_sem=sems[0].at[at], recv_sem=sems[1].at[at],
        device_id=device, device_id_type=MESH,
    )


def started(copies):
    for copy in copies:
        copy.start()
    return copies


HALF = WIDTH // 2
SIDES = ((1, 3, 0), (NY - 1, NY - 3, HALF))


class Scan:
    def __init__(self, step, src, carry, result, scratch):
        self.step, self.src, self.carry_ref, self.result = step, src, carry, result
        self.buf, self.back, self.total, self.group, self.relay = scratch[:5]
        sems = [scratch[i:i + 2] for i in range(5, 15, 2)]
        self.out_sems, self.back_sems, self.near_sems, self.far_sems, self.group_sems = sems
        self.dp, _, self.z, self.y = place()
        self.out_copies, self.back_copies, self.relay_copies = [], [], []
        self.order = range(NY) if step > 0 else range(NY - 1, -1, -1)

    def around(self, k):
        return lax.rem(self.y + k, NY)

    def at_y(self, k):
        return (self.dp, self.z * NY + self.around(k))

    def carry(self, j):
        return self.carry_ref[pl.ds(j, 1), :]

    def block(self, j):
        return self.buf[lax.rem(self.y - j + NY, NY)]

    def half_way(self, phase):
        src = (self.src, self.back)[phase].at[self.around(NY // 2)]
        for side, (near, _, row) in enumerate(SIDES):
            at = 2 * phase + side
            self.relay_copies += started([
                send(src.at[pl.ds(row, HALF)], self.relay.at[at], self.near_sems, at, self.at_y(near))
            ])

    def pass_on(self, phase):
        for copy in self.relay_copies[-2:]:
            copy.wait_recv()
        for side, (near, far, row) in enumerate(SIDES):
            at = 2 * phase + side
            slot = self.result.at[self.around(NY - near)] if phase else self.buf.at[NY // 2]
            self.relay_copies += started([
                send(self.relay.at[at], slot.at[pl.ds(row, HALF)], self.far_sems, at, self.at_y(far))
            ])

    def half_way_arrived(self, phase):
        for side, (_, far, row) in enumerate(SIDES):
            at = 2 * phase + side
            slot = self.result.at[self.around(NY // 2)] if phase else self.buf.at[NY // 2]
            send(
                self.relay.at[at], slot.at[pl.ds(row, HALF)], self.far_sems, at, self.at_y(far)
            ).wait_recv()

    def scatter(self, offsets):
        self.out_copies += started([
            send(self.src.at[self.around(k)], self.buf.at[k], self.out_sems, k, self.at_y(k))
            for k in offsets
        ])

    def group_copy(self, far):
        there = (self.dp, (self.z + self.step * far) * NY + self.y)
        return send(self.total, self.group.at[far - 1], self.group_sems, far - 1, there)

    def has(self, far):
        other = self.z + far
        return (other >= 0) & (other < NZL)

    def totals(self):
        self.buf[0] = self.src[self.y]
        for copy in self.out_copies:
            copy.wait_recv()
        self.half_way_arrived(0)
        total = jnp.zeros((WIDTH, WIDTH), f32)
        for j in self.order:
            total = self.carry(j) * total + self.block(j)
        self.total[...] = total
        for far in (1, 2):
            pl.when(self.has(self.step * far))(lambda far=far: self.group_copy(far).start())

    def combine(self):
        for far in (1, 2):
            source = self.has(-self.step * far)
            pl.when(source)(lambda far=far: self.group_copy(far).wait_recv())

            @pl.when(jnp.logical_not(source))
            def _():
                self.group[far - 1] = jnp.zeros((WIDTH, WIDTH), f32)

        now = self.group[0] + self.carry(8 if self.step > 0 else 9) * self.group[1]
        for j in self.order:
            self.back[j] = now
            now = self.carry(j) * now + self.block(j)

    def give_back(self, offsets):
        self.back_copies += started([
            send(self.back.at[self.around(k)], self.result.at[self.y], self.back_sems, k, self.at_y(k))
            for k in offsets
        ])

    def arrive(self):
        self.result[self.y] = self.back[self.y]
        for k in DIRECT:
            send(
                self.back.at[0], self.result.at[self.around(NY - k)], self.back_sems, k, self.at_y(k)
            ).wait_recv()
        self.half_way_arrived(1)

    def finish(self):
        for far in (1, 2):
            pl.when(self.has(self.step * far))(lambda far=far: self.group_copy(far).wait_send())
        for copy in self.out_copies + self.back_copies + self.relay_copies:
            copy.wait_send()


FAR, NEAR = (3, 5), (2, 6, 1, 7)
DIRECT = FAR + NEAR
HEADS_BUF = pltpu.VMEM((HEADS, WIDTH, WIDTH), f32)
SCAN_SCRATCH = [
    HEADS_BUF, HEADS_BUF, pltpu.VMEM((WIDTH, WIDTH), f32), pltpu.VMEM((2, WIDTH, WIDTH), f32),
    pltpu.VMEM((4, HALF, WIDTH), f32),
] + [pltpu.SemaphoreType.DMA((NY,))] * 4 + [pltpu.SemaphoreType.DMA((4,))] * 4 + [pltpu.SemaphoreType.DMA((2,))] * 2


def attention_part(
    q_ref, k_ref, v_ref, layer_ref, gain_ref, rate_ref, len_ref, in_ref,
    px_ref, pz_ref, attention_buf, normed_buf,
):
    base = lax.axis_index("ctx") * ROWS
    bounds = doc_bounds(len_ref)
    offsets, entering, _ = edge_tables(base, bounds)
    same, distance = pair_tables(base, bounds)
    for h in range(HEADS):
        cols = pl.ds(h * WIDTH, WIDTH)
        rate = rate_ref[h]
        q, k, v = q_ref[:, cols], k_ref[:, cols], v_ref[:, cols]
        mask = jnp.where(same, jnp.exp(-rate * distance), 0.0)
        entry = jnp.where(entering, jnp.exp(-rate * offsets), 0.0)
        s_high, s_low = split(matmul(q, k, NT) * mask)
        in_high, in_low = split(in_ref[h])
        attention = matmul(s_high, v, NN) + matmul(s_low, v, NN)
        attention += entry * (matmul(q, in_high, NN) + matmul(q, in_low, NN))
        attention_buf[:, cols] = attention
    attention = attention_buf[...]
    mean = jnp.mean(attention * attention, axis=-1, keepdims=True)
    normed_buf[...] = (attention * lax.rsqrt(mean + norm_eps) * gain_ref[...]).astype(bf16)
    for h in range(HEADS):
        x, z_high = h // 2, h % 2
        product = matmul(normed_buf[:, pl.ds(h * WIDTH, WIDTH)], layer_ref[...], TN)
        for core in range(2):
            px_ref[x, z_high, core] = product[core * 64:core * 64 + 64, :XCOLS]
            for z_low in range(NZL):
                row = core * 64 + z_low * 16
                pz_ref[z_high * 4 + z_low, core, x] = product[row:row + 16, XCOLS:]


def pair_tables(base, bounds):
    rows = lax.broadcasted_iota(jnp.int32, (ROWS, ROWS), 0)
    columns = lax.broadcasted_iota(jnp.int32, (ROWS, ROWS), 1)
    same = (doc_of(base + rows, bounds) == doc_of(base + columns, bounds)) & (rows >= columns)
    return same, jnp.maximum(rows - columns, 0).astype(f32)


def block_part(q_ref, k_ref, v_ref, g_ref, rate_ref, len_ref, in_ref, dq_ref, dk_ref, dv_ref):
    base = lax.axis_index("ctx") * ROWS
    bounds = doc_bounds(len_ref)
    offsets, entering, _ = edge_tables(base, bounds)
    same, distance = pair_tables(base, bounds)
    for h in range(HEADS):
        cols = pl.ds(h * WIDTH, WIDTH)
        rate = rate_ref[h]
        q, k, v, g = q_ref[:, cols], k_ref[:, cols], v_ref[:, cols], g_ref[:, cols]
        mask = jnp.where(same, jnp.exp(-rate * distance), 0.0)
        entry = jnp.where(entering, jnp.exp(-rate * offsets), 0.0)
        s_high, s_low = split(matmul(q, k, NT) * mask)
        d_high, d_low = split(matmul(g, v, NT) * mask)
        in_high, in_low = split(in_ref[h])
        dq = matmul(d_high, k, NN) + matmul(d_low, k, NN)
        dq += entry * (matmul(g, in_high, NT) + matmul(g, in_low, NT))
        dq_ref[:, cols] = dq.astype(bf16)
        dk_ref[:, cols] = matmul(d_high, q, TN) + matmul(d_low, q, TN)
        dv_ref[:, cols] = matmul(s_high, g, TN) + matmul(s_low, g, TN)


def gradients_kernel(
    k_ref, v_ref, rate_ref, len_ref, grad_ref, dq_part, dk_part, dv_part, dq_ref, dk_ref, dv_ref,
):
    offsets, _, leaving = edge_tables(lax.axis_index("ctx") * ROWS, doc_bounds(len_ref))
    dq_ref[...] = dq_part[...]
    for h in range(HEADS):
        cols = pl.ds(h * WIDTH, WIDTH)
        k, v = k_ref[:, cols], v_ref[:, cols]
        leave = jnp.where(leaving, jnp.exp(-rate_ref[h] * (ROWS - offsets)), 0.0)
        grad_high, grad_low = split(grad_ref[h])
        dk = leave * (matmul(v, grad_high, NT) + matmul(v, grad_low, NT))
        dk_ref[:, cols] = (dk_part[:, cols] + dk).astype(bf16)
        dv = leave * (matmul(k, grad_high, NN) + matmul(k, grad_low, NN))
        dv_ref[:, cols] = (dv_part[:, cols] + dv).astype(bf16)


def main_kernel(
    scale, q_ref, k_ref, v_ref, g_ref, layer_ref, gain_ref, rate_ref, len_ref,
    out_ref, grad_ref, dq_ref, dk_ref, dv_ref,
    state_ref, pull_ref, carry_ref, in_ref, px_ref, pz_ref, attention_buf, normed_buf, cx_buf, ax_buf, x_buf, bx_buf, xz_buf, cz_buf, az_buf, z_buf, bz_buf, zx_buf, c_buf, y_buf,
    core_send, core_recv, x_send, x_recv, xz_send, xz_recv,
    z_send, z_recv, zx_send, zx_recv, y_send, y_recv, *scratch,
):
    dp, ctx, z_low, y = place()
    x, z_high, core = dp // 4, lax.rem(dp // 2, 2), lax.rem(dp, 2)
    z = z_high * 4 + z_low
    twin = (dp + 1 - 2 * core, ctx)

    def at_x(k):
        return (lax.rem(x + k, NX) * 4 + lax.rem(dp, 4), ctx)

    def at_z(k):
        there = lax.rem(z + k, NZ)
        return (x * 4 + there // 4 * 2 + core, lax.rem(there, 4) * NY + y)

    def at_y(k):
        return (dp, ctx - y + lax.rem(y + k, NY))

    ahead = Scan(1, state_ref, carry_ref, in_ref, scratch[:15])
    scan = Scan(-1, pull_ref, carry_ref, grad_ref, scratch[15:])
    partners = (
        [twin] + [at_x(k) for k in range(1, NX)] + [at_z(k) for k in range(1, NZ)]
        + [at_y(k) for k in range(1, NY)]
    )
    barrier = pltpu.get_barrier_semaphore()
    for device in partners:
        pl.semaphore_signal(barrier, inc=1, device_id=device, device_id_type=MESH)
    state_part(k_ref, v_ref, rate_ref, len_ref, state_ref, carry_ref)
    pl.semaphore_wait(barrier, len(partners))
    ahead.half_way(0)
    ahead.scatter(DIRECT)
    pull_part(q_ref, g_ref, rate_ref, len_ref, pull_ref)
    ahead.pass_on(0)
    ahead.totals()
    scan.half_way(0)
    scan.scatter(NEAR)
    ahead.combine()
    ahead.half_way(1)
    ahead.give_back(DIRECT)
    scan.pass_on(0)
    ahead.pass_on(1)
    scan.scatter(FAR)
    ahead.arrive()
    attention_part(
        q_ref, k_ref, v_ref, layer_ref, gain_ref, rate_ref, len_ref, in_ref,
        px_ref, pz_ref, attention_buf, normed_buf,
    )
    core_sems = (core_send, core_recv)
    order = tuple(range(1, NX)) + (0,)
    core_copies = started(
        [send(pz_ref.at[:, 1 - core], cz_buf, core_sems, NX, twin)]
        + [
            send(px_ref.at[lax.rem(x + k, NX), :, 1 - core], cx_buf.at[k], core_sems, k, twin)
            for k in order
        ]
    )
    core_copies[0].wait_recv()
    az_buf[...] = pz_ref[:, core] + cz_buf[...]
    z_copies = started([
        send(az_buf.at[lax.rem(z + k, NZ)], z_buf.at[k], (z_send, z_recv), k, at_z(k))
        for k in range(1, NZ)
    ])
    x_copies = []
    for k, copy in zip(order, core_copies[1:]):
        copy.wait_recv()
        ax_buf[k] = px_ref[lax.rem(x + k, NX), :, core] + cx_buf[k]
        if k:
            x_copies += started([send(ax_buf.at[k], x_buf.at[k], (x_send, x_recv), k, at_x(k))])

    block_part(q_ref, k_ref, v_ref, g_ref, rate_ref, len_ref, in_ref, dq_ref, dk_ref, dv_ref)
    scan.totals()

    def gather(total, copies, buf):
        for k, copy in enumerate(copies, 1):
            copy.wait_recv()
            total = total + buf[k]
        return total

    bx_buf[...] = gather(ax_buf[0], x_copies, x_buf).reshape(bx_buf.shape)
    xz_copies = started([
        send(bx_buf.at[lax.rem(z + k, NZ)], xz_buf.at[k], (xz_send, xz_recv), k, at_z(k))
        for k in range(1, NZ)
    ])
    scan.combine()
    scan.half_way(1)
    scan.give_back(FAR)
    bz_buf[...] = gather(az_buf[z], z_copies, z_buf)
    zx_copies = started([
        send(bz_buf.at[lax.rem(x + k, NX)], zx_buf.at[k], (zx_send, zx_recv), k, at_x(k))
        for k in range(1, NX)
    ])
    scan.pass_on(1)
    right = gather(bz_buf[x], zx_copies, zx_buf)
    left = gather(bx_buf[z], xz_copies, xz_buf)
    for j in range(NY):
        c_buf[j, :, :XCOLS] = left[2 * j:2 * j + 2, :]
        c_buf[j, :, XCOLS:] = right[2 * j:2 * j + 2, :]
    y_copies = started([
        send(c_buf.at[lax.rem(y + k, NY)], y_buf.at[k], (y_send, y_recv), k, at_y(k))
        for k in range(1, NY)
    ])
    scan.give_back(NEAR)
    out_ref[...] = gather(c_buf[y], y_copies, y_buf) * scale
    scan.arrive()
    scan.finish()
    ahead.finish()
    for copy in core_copies + x_copies + z_copies + xz_copies + zx_copies + y_copies:
        copy.wait_send()


def on_device(queries, keys, values, out_grad, layer_grad, norm_gain, decay_rates, doc_lengths):
    rows, features, bucket = ROWS, HEADS * WIDTH, layer_grad.shape[2]
    scale = 1.0 / math.sqrt(rows * lax.axis_size("dp") * lax.axis_size("ctx"))
    q, k, v, g = (a.reshape(rows, features) for a in (queries, keys, values, out_grad))
    layer = layer_grad.reshape(rows, bucket)
    states = jax.ShapeDtypeStruct((HEADS, WIDTH, WIDTH), f32)
    zcols = bucket - XCOLS
    dma = pltpu.SemaphoreType.DMA
    part = jax.ShapeDtypeStruct((rows, features), f32)
    grad_shape = jax.ShapeDtypeStruct((rows, features), bf16)
    proj_grad, state_grad, *parts = pl.pallas_call(
        functools.partial(main_kernel, scale),
        out_shape=(jax.ShapeDtypeStruct((2, bucket), f32), states, grad_shape, part, part),
        in_specs=[VMEM_SPEC] * 6 + [SMEM_SPEC] * 2,
        out_specs=(VMEM_SPEC,) * 5,
        scratch_shapes=[
            HEADS_BUF,
            HEADS_BUF,
            pltpu.VMEM((16, WIDTH), f32),
            HEADS_BUF,
            pltpu.VMEM((NX, 2, 2, 64, XCOLS), f32),
            pltpu.VMEM((NZ, 2, NX, 16, zcols), f32),
            pltpu.VMEM((rows, features), f32),
            pltpu.VMEM((rows, features), bf16),
        ]
        + [pltpu.VMEM((NX, 2, 64, XCOLS), f32)] * 3
        + [pltpu.VMEM((NZ, 16, XCOLS), f32)] * 2
        + [pltpu.VMEM((NZ, NX, 16, zcols), f32)] * 3
        + [pltpu.VMEM((NX, 16, zcols), f32)] * 2
        + [pltpu.VMEM((NY, 2, bucket), f32)] * 2
        + [dma((NX + 1,))] * 2 + [dma((NX,))] * 2 + [dma((NZ,))] * 4
        + [dma((NX,))] * 2 + [dma((NY,))] * 2
        + SCAN_SCRATCH * 2,
        compiler_params=pltpu.CompilerParams(collective_id=0, has_side_effects=True),
        name="main",
    )(q, k, v, g, layer, norm_gain.reshape(1, features), decay_rates, doc_lengths)
    query_grad, key_grad, value_grad = pl.pallas_call(
        gradients_kernel,
        out_shape=(grad_shape,) * 3,
        in_specs=[VMEM_SPEC] * 2 + [SMEM_SPEC] * 2 + [VMEM_SPEC] * 4,
        out_specs=(VMEM_SPEC,) * 3,
        name="gradients",
    )(k, v, decay_rates, doc_lengths, state_grad, *parts)
    shape_out = (1, rows, features)
    return (
        query_grad.reshape(shape_out),
        key_grad.reshape(shape_out),
        value_grad.reshape(shape_out),
        proj_grad,
    )


def solution(mesh):
    block = P("dp", "ctx", None)
    return jax.shard_map(
        on_device,
        mesh=mesh,
        in_specs=(block,) * 5 + (P(), P(), P("dp", None)),
        out_specs=(block,) * 3 + (P(("dp", "ctx"), None),),
        check_vma=False,
    )
```

```python
import functools
import math

import jax
import jax.numpy as jnp
from jax import lax
from jax.experimental import pallas as pl
from jax.experimental.pallas import tpu as pltpu
from jax.sharding import PartitionSpec as P

norm_eps = 1e-06
HEADS, WIDTH, ROWS = 8, 128, 128
NX, NZ, NY, NZL = 4, 8, 8, 4
XCOLS = 512
MESH = pl.DeviceIdType.MESH
f32, bf16 = jnp.float32, jnp.bfloat16
VMEM_SPEC = pl.BlockSpec(memory_space=pltpu.VMEM)
SMEM_SPEC = pl.BlockSpec(memory_space=pltpu.SMEM)


def split(value):
    high = value.astype(bf16)
    return high, (value - high.astype(f32)).astype(bf16)


def matmul(a, b, dims):
    return lax.dot_general(a, b, (dims, ((), ())), preferred_element_type=f32)


NN, NT, TN = ((1,), (0,)), ((1,), (1,)), ((0,), (0,))


def doc_bounds(len_ref):
    first = len_ref[0, 0]
    second = first + len_ref[0, 1]
    return first, second, second + len_ref[0, 2]


def doc_of(positions, bounds):
    return sum((positions >= bound).astype(jnp.int32) for bound in bounds)


def doc_of_scalar(position, bounds):
    return sum(jnp.where(position >= bound, 1, 0) for bound in bounds)


def edge_tables(base, bounds):
    offsets = lax.broadcasted_iota(jnp.int32, (ROWS, WIDTH), 0)
    docs = doc_of(base + offsets, bounds)
    entering = docs == doc_of_scalar(base - 1, bounds)
    leaving = docs == doc_of_scalar(base + ROWS - 1, bounds)
    return offsets.astype(f32), entering, leaving


def state_part(k_ref, v_ref, rate_ref, len_ref, state_ref, carry_ref):
    ctx = lax.axis_index("ctx")
    bounds = doc_bounds(len_ref)
    offsets, _, leaving = edge_tables(ctx * ROWS, bounds)
    for h in range(HEADS):
        cols = pl.ds(h * WIDTH, WIDTH)
        leave = jnp.where(leaving, jnp.exp(-rate_ref[h] * (ROWS - offsets)), 0.0)
        high, low = split(k_ref[:, cols].astype(f32) * leave)
        v = v_ref[:, cols]
        state_ref[h] = matmul(high, v, TN) + matmul(low, v, TN)
    group, own = ctx // NY, lax.rem(ctx, NY)
    rate = rate_ref[own]

    def carry(first, blocks):
        start = first * ROWS
        whole = doc_of_scalar(start - 1, bounds) == doc_of_scalar(start + blocks * ROWS - 1, bounds)
        decay = jnp.exp(jnp.full((1, WIDTH), -rate * float(blocks * ROWS), f32))
        return jnp.where(whole, decay, 0.0)

    for j in range(NY):
        carry_ref[pl.ds(j, 1), :] = carry(group * NY + j, 1)
    carry_ref[pl.ds(8, 1), :] = carry((group - 1) * NY, NY)
    carry_ref[pl.ds(9, 1), :] = carry((group + 1) * NY, NY)


def pull_part(q_ref, g_ref, rate_ref, len_ref, pull_ref):
    offsets, entering, _ = edge_tables(lax.axis_index("ctx") * ROWS, doc_bounds(len_ref))
    for h in range(HEADS):
        cols = pl.ds(h * WIDTH, WIDTH)
        entry = jnp.where(entering, jnp.exp(-rate_ref[h] * offsets), 0.0)
        high, low = split(q_ref[:, cols].astype(f32) * entry)
        g = g_ref[:, cols]
        pull_ref[h] = matmul(high, g, TN) + matmul(low, g, TN)


def place():
    dp, ctx = lax.axis_index("dp"), lax.axis_index("ctx")
    return dp, ctx, ctx // NY, lax.rem(ctx, NY)


def send(src, dst, sems, at, device):
    return pltpu.make_async_remote_copy(
        src_ref=src, dst_ref=dst, send_sem=sems[0].at[at], recv_sem=sems[1].at[at],
        device_id=device, device_id_type=MESH,
    )


def started(copies):
    for copy in copies:
        copy.start()
    return copies


HALF = WIDTH // 2
SIDES = ((1, 3, 0), (NY - 1, NY - 3, HALF))


class Scan:
    def __init__(self, step, src, carry, result, scratch):
        self.step, self.src, self.carry_ref, self.result = step, src, carry, result
        self.buf, self.back, self.total, self.group, self.relay = scratch[:5]
        sems = [scratch[i:i + 2] for i in range(5, 15, 2)]
        self.out_sems, self.back_sems, self.near_sems, self.far_sems, self.group_sems = sems
        self.dp, _, self.z, self.y = place()
        self.out_copies, self.back_copies, self.relay_copies = [], [], []
        self.order = range(NY) if step > 0 else range(NY - 1, -1, -1)

    def around(self, k):
        return lax.rem(self.y + k, NY)

    def at_y(self, k):
        return (self.dp, self.z * NY + self.around(k))

    def carry(self, j):
        return self.carry_ref[pl.ds(j, 1), :]

    def block(self, j):
        return self.buf[lax.rem(self.y - j + NY, NY)]

    def half_way(self, phase):
        src = (self.src, self.back)[phase].at[self.around(NY // 2)]
        for side, (near, _, row) in enumerate(SIDES):
            at = 2 * phase + side
            self.relay_copies += started([
                send(src.at[pl.ds(row, HALF)], self.relay.at[at], self.near_sems, at, self.at_y(near))
            ])

    def pass_on(self, phase):
        for copy in self.relay_copies[-2:]:
            copy.wait_recv()
        for side, (near, far, row) in enumerate(SIDES):
            at = 2 * phase + side
            slot = self.result.at[self.around(NY - near)] if phase else self.buf.at[NY // 2]
            self.relay_copies += started([
                send(self.relay.at[at], slot.at[pl.ds(row, HALF)], self.far_sems, at, self.at_y(far))
            ])

    def half_way_arrived(self, phase):
        for side, (_, far, row) in enumerate(SIDES):
            at = 2 * phase + side
            slot = self.result.at[self.around(NY // 2)] if phase else self.buf.at[NY // 2]
            send(
                self.relay.at[at], slot.at[pl.ds(row, HALF)], self.far_sems, at, self.at_y(far)
            ).wait_recv()

    def scatter(self, offsets):
        self.out_copies += started([
            send(self.src.at[self.around(k)], self.buf.at[k], self.out_sems, k, self.at_y(k))
            for k in offsets
        ])

    def group_copy(self, far):
        there = (self.dp, (self.z + self.step * far) * NY + self.y)
        return send(self.total, self.group.at[far - 1], self.group_sems, far - 1, there)

    def has(self, far):
        other = self.z + far
        return (other >= 0) & (other < NZL)

    def totals(self):
        self.buf[0] = self.src[self.y]
        for copy in self.out_copies:
            copy.wait_recv()
        self.half_way_arrived(0)
        total = jnp.zeros((WIDTH, WIDTH), f32)
        for j in self.order:
            total = self.carry(j) * total + self.block(j)
        self.total[...] = total
        for far in (1, 2):
            pl.when(self.has(self.step * far))(lambda far=far: self.group_copy(far).start())

    def combine(self):
        for far in (1, 2):
            source = self.has(-self.step * far)
            pl.when(source)(lambda far=far: self.group_copy(far).wait_recv())

            @pl.when(jnp.logical_not(source))
            def _():
                self.group[far - 1] = jnp.zeros((WIDTH, WIDTH), f32)

        now = self.group[0] + self.carry(8 if self.step > 0 else 9) * self.group[1]
        for j in self.order:
            self.back[j] = now
            now = self.carry(j) * now + self.block(j)

    def give_back(self, offsets):
        self.back_copies += started([
            send(self.back.at[self.around(k)], self.result.at[self.y], self.back_sems, k, self.at_y(k))
            for k in offsets
        ])

    def arrive(self):
        self.result[self.y] = self.back[self.y]
        for k in DIRECT:
            send(
                self.back.at[0], self.result.at[self.around(NY - k)], self.back_sems, k, self.at_y(k)
            ).wait_recv()
        self.half_way_arrived(1)

    def finish(self):
        for far in (1, 2):
            pl.when(self.has(self.step * far))(lambda far=far: self.group_copy(far).wait_send())
        for copy in self.out_copies + self.back_copies + self.relay_copies:
            copy.wait_send()


FAR, NEAR = (3, 5), (2, 6, 1, 7)
DIRECT = FAR + NEAR
HEADS_BUF = pltpu.VMEM((HEADS, WIDTH, WIDTH), f32)
SCAN_SCRATCH = [
    HEADS_BUF, HEADS_BUF, pltpu.VMEM((WIDTH, WIDTH), f32), pltpu.VMEM((2, WIDTH, WIDTH), f32),
    pltpu.VMEM((4, HALF, WIDTH), f32),
] + [pltpu.SemaphoreType.DMA((NY,))] * 4 + [pltpu.SemaphoreType.DMA((4,))] * 4 + [pltpu.SemaphoreType.DMA((2,))] * 2


def attention_block(q_ref, k_ref, v_ref, rate_ref, len_ref, attention_buf):
    base = lax.axis_index("ctx") * ROWS
    same, distance = pair_tables(base, doc_bounds(len_ref))
    for h in range(HEADS):
        cols = pl.ds(h * WIDTH, WIDTH)
        v = v_ref[:, cols]
        mask = jnp.where(same, jnp.exp(-rate_ref[h] * distance), 0.0)
        s_high, s_low = split(matmul(q_ref[:, cols], k_ref[:, cols], NT) * mask)
        attention_buf[:, cols] = matmul(s_high, v, NN) + matmul(s_low, v, NN)


def attention_rest(q_ref, gain_ref, rate_ref, len_ref, in_ref, attention_buf, normed_buf):
    offsets, entering, _ = edge_tables(lax.axis_index("ctx") * ROWS, doc_bounds(len_ref))
    for h in range(HEADS):
        cols = pl.ds(h * WIDTH, WIDTH)
        q = q_ref[:, cols]
        entry = jnp.where(entering, jnp.exp(-rate_ref[h] * offsets), 0.0)
        in_high, in_low = split(in_ref[h])
        attention_buf[:, cols] += entry * (matmul(q, in_high, NN) + matmul(q, in_low, NN))
    attention = attention_buf[...]
    mean = jnp.mean(attention * attention, axis=-1, keepdims=True)
    normed_buf[...] = (attention * lax.rsqrt(mean + norm_eps) * gain_ref[...]).astype(bf16)


def pair_tables(base, bounds):
    rows = lax.broadcasted_iota(jnp.int32, (ROWS, ROWS), 0)
    columns = lax.broadcasted_iota(jnp.int32, (ROWS, ROWS), 1)
    same = (doc_of(base + rows, bounds) == doc_of(base + columns, bounds)) & (rows >= columns)
    return same, jnp.maximum(rows - columns, 0).astype(f32)


def block_part(q_ref, k_ref, v_ref, g_ref, rate_ref, len_ref, in_ref, dq_ref, dk_ref, dv_ref):
    base = lax.axis_index("ctx") * ROWS
    bounds = doc_bounds(len_ref)
    offsets, entering, _ = edge_tables(base, bounds)
    same, distance = pair_tables(base, bounds)
    for h in range(HEADS):
        cols = pl.ds(h * WIDTH, WIDTH)
        rate = rate_ref[h]
        q, k, v, g = q_ref[:, cols], k_ref[:, cols], v_ref[:, cols], g_ref[:, cols]
        mask = jnp.where(same, jnp.exp(-rate * distance), 0.0)
        entry = jnp.where(entering, jnp.exp(-rate * offsets), 0.0)
        s_high, s_low = split(matmul(q, k, NT) * mask)
        d_high, d_low = split(matmul(g, v, NT) * mask)
        in_high, in_low = split(in_ref[h])
        dq = matmul(d_high, k, NN) + matmul(d_low, k, NN)
        dq += entry * (matmul(g, in_high, NT) + matmul(g, in_low, NT))
        dq_ref[:, cols] = dq.astype(bf16)
        dk_ref[:, cols] = matmul(d_high, q, TN) + matmul(d_low, q, TN)
        dv_ref[:, cols] = matmul(s_high, g, TN) + matmul(s_low, g, TN)


def gradients_kernel(
    k_ref, v_ref, rate_ref, len_ref, grad_ref, dq_part, dk_part, dv_part, dq_ref, dk_ref, dv_ref,
):
    offsets, _, leaving = edge_tables(lax.axis_index("ctx") * ROWS, doc_bounds(len_ref))
    dq_ref[...] = dq_part[...]
    for h in range(HEADS):
        cols = pl.ds(h * WIDTH, WIDTH)
        k, v = k_ref[:, cols], v_ref[:, cols]
        leave = jnp.where(leaving, jnp.exp(-rate_ref[h] * (ROWS - offsets)), 0.0)
        grad_high, grad_low = split(grad_ref[h])
        dk = leave * (matmul(v, grad_high, NT) + matmul(v, grad_low, NT))
        dk_ref[:, cols] = (dk_part[:, cols] + dk).astype(bf16)
        dv = leave * (matmul(k, grad_high, NN) + matmul(k, grad_low, NN))
        dv_ref[:, cols] = (dv_part[:, cols] + dv).astype(bf16)


def main_kernel(
    scale, q_ref, k_ref, v_ref, g_ref, layer_ref, gain_ref, rate_ref, len_ref,
    out_ref, grad_ref, dq_ref, dk_ref, dv_ref,
    state_ref, pull_ref, carry_ref, in_ref, px_ref, pz_ref, attention_buf, normed_buf, cx_buf, ax_buf, x_buf, bx_buf, xz_buf, cz_buf, az_buf, z_buf, bz_buf, zx_buf, c_buf, y_buf,
    core_send, core_recv, x_send, x_recv, xz_send, xz_recv,
    z_send, z_recv, zx_send, zx_recv, y_send, y_recv, *scratch,
):
    dp, ctx, z_low, y = place()
    x, z_high, core = dp // 4, lax.rem(dp // 2, 2), lax.rem(dp, 2)
    z = z_high * 4 + z_low
    twin = (dp + 1 - 2 * core, ctx)

    def at_x(k):
        return (lax.rem(x + k, NX) * 4 + lax.rem(dp, 4), ctx)

    def at_z(k):
        there = lax.rem(z + k, NZ)
        return (x * 4 + there // 4 * 2 + core, lax.rem(there, 4) * NY + y)

    def at_y(k):
        return (dp, ctx - y + lax.rem(y + k, NY))

    ahead = Scan(1, state_ref, carry_ref, in_ref, scratch[:15])
    scan = Scan(-1, pull_ref, carry_ref, grad_ref, scratch[15:])
    partners = (
        [twin] + [at_x(k) for k in range(1, NX)] + [at_z(k) for k in range(1, NZ)]
        + [at_y(k) for k in range(1, NY)]
    )
    barrier = pltpu.get_barrier_semaphore()
    for device in partners:
        pl.semaphore_signal(barrier, inc=1, device_id=device, device_id_type=MESH)
    state_part(k_ref, v_ref, rate_ref, len_ref, state_ref, carry_ref)
    pl.semaphore_wait(barrier, len(partners))
    ahead.half_way(0)
    ahead.scatter(DIRECT)
    pull_part(q_ref, g_ref, rate_ref, len_ref, pull_ref)
    ahead.pass_on(0)
    attention_block(q_ref, k_ref, v_ref, rate_ref, len_ref, attention_buf)
    ahead.totals()
    scan.half_way(0)
    scan.scatter(NEAR)
    ahead.combine()
    ahead.half_way(1)
    ahead.give_back(DIRECT)
    scan.pass_on(0)
    ahead.pass_on(1)
    scan.scatter(FAR)
    ahead.arrive()
    attention_rest(q_ref, gain_ref, rate_ref, len_ref, in_ref, attention_buf, normed_buf)

    def product(block, columns):
        features = pl.ds(pl.multiple_of(block * WIDTH, WIDTH), WIDTH)
        return matmul(normed_buf[:, features], layer_ref[:, columns], TN)

    for h in range(HEADS):
        rows = product(h, slice(XCOLS, None))
        for half in range(2):
            for low in range(NZL):
                row = half * 64 + low * 16
                pz_ref[h % 2 * 4 + low, half, h // 2] = rows[row:row + 16]
    core_sems = (core_send, core_recv)
    core_copies = started([send(pz_ref.at[:, 1 - core], cz_buf, core_sems, NX, twin)])

    def to_twin(k):
        there = lax.rem(x + k, NX)
        for high in range(2):
            rows = product(there * 2 + high, slice(0, XCOLS))
            for half in range(2):
                px_ref[there, high, half] = rows[half * 64:half * 64 + 64]
        core_copies.extend(
            started([send(px_ref.at[there, :, 1 - core], cx_buf.at[k], core_sems, k, twin)])
        )

    def to_z(offsets):
        return started([
            send(az_buf.at[lax.rem(z + k, NZ)], z_buf.at[k], (z_send, z_recv), k, at_z(k))
            for k in offsets
        ])

    order = tuple(range(1, NX)) + (0,)
    for k in order[:2]:
        to_twin(k)
    core_copies[0].wait_recv()
    az_buf[...] = pz_ref[:, core] + cz_buf[...]
    z_copies = to_z((3, 4, 5))
    for k in order[2:]:
        to_twin(k)
    x_copies = []
    for k, copy in zip(order, core_copies[1:]):
        copy.wait_recv()
        ax_buf[k] = px_ref[lax.rem(x + k, NX), :, core] + cx_buf[k]
        if k:
            x_copies += started([send(ax_buf.at[k], x_buf.at[k], (x_send, x_recv), k, at_x(k))])
    scan.totals()
    z_copies = to_z((1, 2)) + z_copies + to_z((6, 7))
    block_part(q_ref, k_ref, v_ref, g_ref, rate_ref, len_ref, in_ref, dq_ref, dk_ref, dv_ref)
    scan.combine()
    scan.half_way(1)
    scan.give_back(DIRECT)

    def gather(total, copies, buf):
        for k, copy in enumerate(copies, 1):
            copy.wait_recv()
            total = total + buf[k]
        return total

    bx_buf[...] = gather(ax_buf[0], x_copies, x_buf).reshape(bx_buf.shape)
    xz_copies = started([
        send(bx_buf.at[lax.rem(z + k, NZ)], xz_buf.at[k], (xz_send, xz_recv), k, at_z(k))
        for k in range(1, NZ)
    ])
    scan.pass_on(1)
    bz_buf[...] = gather(az_buf[z], z_copies, z_buf)
    zx_copies = started([
        send(bz_buf.at[lax.rem(x + k, NX)], zx_buf.at[k], (zx_send, zx_recv), k, at_x(k))
        for k in range(1, NX)
    ])
    right = gather(bz_buf[x], zx_copies, zx_buf)
    left = gather(bx_buf[z], xz_copies, xz_buf)
    for j in range(NY):
        c_buf[j, :, :XCOLS] = left[2 * j:2 * j + 2, :]
        c_buf[j, :, XCOLS:] = right[2 * j:2 * j + 2, :]
    y_copies = started([
        send(c_buf.at[lax.rem(y + k, NY)], y_buf.at[k], (y_send, y_recv), k, at_y(k))
        for k in range(1, NY)
    ])
    out_ref[...] = gather(c_buf[y], y_copies, y_buf) * scale
    scan.arrive()
    scan.finish()
    ahead.finish()
    for copy in core_copies + x_copies + z_copies + xz_copies + zx_copies + y_copies:
        copy.wait_send()


def on_device(queries, keys, values, out_grad, layer_grad, norm_gain, decay_rates, doc_lengths):
    rows, features, bucket = ROWS, HEADS * WIDTH, layer_grad.shape[2]
    scale = 1.0 / math.sqrt(rows * lax.axis_size("dp") * lax.axis_size("ctx"))
    q, k, v, g = (a.reshape(rows, features) for a in (queries, keys, values, out_grad))
    layer = layer_grad.reshape(rows, bucket)
    states = jax.ShapeDtypeStruct((HEADS, WIDTH, WIDTH), f32)
    zcols = bucket - XCOLS
    dma = pltpu.SemaphoreType.DMA
    part = jax.ShapeDtypeStruct((rows, features), f32)
    grad_shape = jax.ShapeDtypeStruct((rows, features), bf16)
    proj_grad, state_grad, *parts = pl.pallas_call(
        functools.partial(main_kernel, scale),
        out_shape=(jax.ShapeDtypeStruct((2, bucket), f32), states, grad_shape, part, part),
        in_specs=[VMEM_SPEC] * 6 + [SMEM_SPEC] * 2,
        out_specs=(VMEM_SPEC,) * 5,
        scratch_shapes=[
            HEADS_BUF,
            HEADS_BUF,
            pltpu.VMEM((16, WIDTH), f32),
            HEADS_BUF,
            pltpu.VMEM((NX, 2, 2, 64, XCOLS), f32),
            pltpu.VMEM((NZ, 2, NX, 16, zcols), f32),
            pltpu.VMEM((rows, features), f32),
            pltpu.VMEM((rows, features), bf16),
        ]
        + [pltpu.VMEM((NX, 2, 64, XCOLS), f32)] * 3
        + [pltpu.VMEM((NZ, 16, XCOLS), f32)] * 2
        + [pltpu.VMEM((NZ, NX, 16, zcols), f32)] * 3
        + [pltpu.VMEM((NX, 16, zcols), f32)] * 2
        + [pltpu.VMEM((NY, 2, bucket), f32)] * 2
        + [dma((NX + 1,))] * 2 + [dma((NX,))] * 2 + [dma((NZ,))] * 4
        + [dma((NX,))] * 2 + [dma((NY,))] * 2
        + SCAN_SCRATCH * 2,
        compiler_params=pltpu.CompilerParams(collective_id=0, has_side_effects=True),
        name="main",
    )(q, k, v, g, layer, norm_gain.reshape(1, features), decay_rates, doc_lengths)
    query_grad, key_grad, value_grad = pl.pallas_call(
        gradients_kernel,
        out_shape=(grad_shape,) * 3,
        in_specs=[VMEM_SPEC] * 2 + [SMEM_SPEC] * 2 + [VMEM_SPEC] * 4,
        out_specs=(VMEM_SPEC,) * 3,
        name="gradients",
    )(k, v, decay_rates, doc_lengths, state_grad, *parts)
    shape_out = (1, rows, features)
    return (
        query_grad.reshape(shape_out),
        key_grad.reshape(shape_out),
        value_grad.reshape(shape_out),
        proj_grad,
    )


def solution(mesh):
    block = P("dp", "ctx", None)
    return jax.shard_map(
        on_device,
        mesh=mesh,
        in_specs=(block,) * 5 + (P(), P(), P("dp", None)),
        out_specs=(block,) * 3 + (P(("dp", "ctx"), None),),
        check_vma=False,
    )
```

```python
import functools
import math

import jax
import jax.numpy as jnp
from jax import lax
from jax.experimental import pallas as pl
from jax.experimental.pallas import tpu as pltpu
from jax.sharding import PartitionSpec as P

norm_eps = 1e-06
HEADS, WIDTH, ROWS = 8, 128, 128
NX, NZ, NY, NZL = 4, 8, 8, 4
XCOLS = 512
MESH = pl.DeviceIdType.MESH
f32, bf16 = jnp.float32, jnp.bfloat16
VMEM_SPEC = pl.BlockSpec(memory_space=pltpu.VMEM)
SMEM_SPEC = pl.BlockSpec(memory_space=pltpu.SMEM)


def split(value):
    high = value.astype(bf16)
    return high, (value - high.astype(f32)).astype(bf16)


def matmul(a, b, dims):
    return lax.dot_general(a, b, (dims, ((), ())), preferred_element_type=f32)


NN, NT, TN = ((1,), (0,)), ((1,), (1,)), ((0,), (0,))


def doc_bounds(len_ref):
    first = len_ref[0, 0]
    second = first + len_ref[0, 1]
    return first, second, second + len_ref[0, 2]


def doc_of(positions, bounds):
    return sum((positions >= bound).astype(jnp.int32) for bound in bounds)


def doc_of_scalar(position, bounds):
    return sum(jnp.where(position >= bound, 1, 0) for bound in bounds)


def edge_tables(base, bounds):
    offsets = lax.broadcasted_iota(jnp.int32, (ROWS, WIDTH), 0)
    docs = doc_of(base + offsets, bounds)
    entering = docs == doc_of_scalar(base - 1, bounds)
    leaving = docs == doc_of_scalar(base + ROWS - 1, bounds)
    return offsets.astype(f32), entering, leaving


def state_part(k_ref, v_ref, rate_ref, len_ref, state_ref, carry_ref):
    ctx = lax.axis_index("ctx")
    bounds = doc_bounds(len_ref)
    offsets, _, leaving = edge_tables(ctx * ROWS, bounds)
    for h in range(HEADS):
        cols = pl.ds(h * WIDTH, WIDTH)
        leave = jnp.where(leaving, jnp.exp(-rate_ref[h] * (ROWS - offsets)), 0.0)
        high, low = split(k_ref[:, cols].astype(f32) * leave)
        v = v_ref[:, cols]
        state_ref[h] = matmul(high, v, TN) + matmul(low, v, TN)
    group, own = ctx // NY, lax.rem(ctx, NY)
    rate = rate_ref[own]

    def carry(first, blocks):
        start = first * ROWS
        whole = doc_of_scalar(start - 1, bounds) == doc_of_scalar(start + blocks * ROWS - 1, bounds)
        decay = jnp.exp(jnp.full((1, WIDTH), -rate * float(blocks * ROWS), f32))
        return jnp.where(whole, decay, 0.0)

    for j in range(NY):
        carry_ref[pl.ds(j, 1), :] = carry(group * NY + j, 1)
    carry_ref[pl.ds(8, 1), :] = carry((group - 1) * NY, NY)
    carry_ref[pl.ds(9, 1), :] = carry((group + 1) * NY, NY)


def pull_part(q_ref, g_ref, rate_ref, len_ref, pull_ref):
    offsets, entering, _ = edge_tables(lax.axis_index("ctx") * ROWS, doc_bounds(len_ref))
    for h in range(HEADS):
        cols = pl.ds(h * WIDTH, WIDTH)
        entry = jnp.where(entering, jnp.exp(-rate_ref[h] * offsets), 0.0)
        high, low = split(q_ref[:, cols].astype(f32) * entry)
        g = g_ref[:, cols]
        pull_ref[h] = matmul(high, g, TN) + matmul(low, g, TN)


def place():
    dp, ctx = lax.axis_index("dp"), lax.axis_index("ctx")
    return dp, ctx, ctx // NY, lax.rem(ctx, NY)


def send(src, dst, sems, at, device):
    return pltpu.make_async_remote_copy(
        src_ref=src, dst_ref=dst, send_sem=sems[0].at[at], recv_sem=sems[1].at[at],
        device_id=device, device_id_type=MESH,
    )


def started(copies):
    for copy in copies:
        copy.start()
    return copies


HALF = WIDTH // 2
SIDES = ((1, 3, 0), (NY - 1, NY - 3, HALF))


class Scan:
    def __init__(self, step, src, carry, result, scratch):
        self.step, self.src, self.carry_ref, self.result = step, src, carry, result
        self.buf, self.back, self.total, self.group, self.relay = scratch[:5]
        sems = [scratch[i:i + 2] for i in range(5, 15, 2)]
        self.out_sems, self.back_sems, self.near_sems, self.far_sems, self.group_sems = sems
        self.dp, _, self.z, self.y = place()
        self.out_copies, self.back_copies, self.relay_copies = [], [], []
        self.order = range(NY) if step > 0 else range(NY - 1, -1, -1)

    def around(self, k):
        return lax.rem(self.y + k, NY)

    def at_y(self, k):
        return (self.dp, self.z * NY + self.around(k))

    def carry(self, j):
        return self.carry_ref[pl.ds(j, 1), :]

    def block(self, j):
        return self.buf[lax.rem(self.y - j + NY, NY)]

    def half_way(self, phase):
        src = (self.src, self.back)[phase].at[self.around(NY // 2)]
        for side, (near, _, row) in enumerate(SIDES):
            at = 2 * phase + side
            self.relay_copies += started([
                send(src.at[pl.ds(row, HALF)], self.relay.at[at], self.near_sems, at, self.at_y(near))
            ])

    def pass_on(self, phase):
        for copy in self.relay_copies[-2:]:
            copy.wait_recv()
        for side, (near, far, row) in enumerate(SIDES):
            at = 2 * phase + side
            slot = self.result.at[self.around(NY - near)] if phase else self.buf.at[NY // 2]
            self.relay_copies += started([
                send(self.relay.at[at], slot.at[pl.ds(row, HALF)], self.far_sems, at, self.at_y(far))
            ])

    def half_way_arrived(self, phase):
        for side, (_, far, row) in enumerate(SIDES):
            at = 2 * phase + side
            slot = self.result.at[self.around(NY // 2)] if phase else self.buf.at[NY // 2]
            send(
                self.relay.at[at], slot.at[pl.ds(row, HALF)], self.far_sems, at, self.at_y(far)
            ).wait_recv()

    def scatter(self, offsets):
        self.out_copies += started([
            send(self.src.at[self.around(k)], self.buf.at[k], self.out_sems, k, self.at_y(k))
            for k in offsets
        ])

    def group_copy(self, far):
        there = (self.dp, (self.z + self.step * far) * NY + self.y)
        return send(self.total, self.group.at[far - 1], self.group_sems, far - 1, there)

    def has(self, far):
        other = self.z + far
        return (other >= 0) & (other < NZL)

    def totals(self):
        self.buf[0] = self.src[self.y]
        for copy in self.out_copies:
            copy.wait_recv()
        self.half_way_arrived(0)
        total = jnp.zeros((WIDTH, WIDTH), f32)
        for j in self.order:
            total = self.carry(j) * total + self.block(j)
        self.total[...] = total
        for far in (1, 2):
            pl.when(self.has(self.step * far))(lambda far=far: self.group_copy(far).start())

    def combine(self):
        for far in (1, 2):
            source = self.has(-self.step * far)
            pl.when(source)(lambda far=far: self.group_copy(far).wait_recv())

            @pl.when(jnp.logical_not(source))
            def _():
                self.group[far - 1] = jnp.zeros((WIDTH, WIDTH), f32)

        now = self.group[0] + self.carry(8 if self.step > 0 else 9) * self.group[1]
        for j in self.order:
            self.back[j] = now
            now = self.carry(j) * now + self.block(j)

    def give_back(self, offsets):
        self.back_copies += started([
            send(self.back.at[self.around(k)], self.result.at[self.y], self.back_sems, k, self.at_y(k))
            for k in offsets
        ])

    def arrive(self, use):
        self.result[self.y] = self.back[self.y]
        use(self.y)
        for k in DIRECT:
            send(
                self.back.at[0], self.result.at[self.around(NY - k)], self.back_sems, k, self.at_y(k)
            ).wait_recv()
            use(self.around(NY - k))
        self.half_way_arrived(1)
        use(self.around(NY // 2))

    def finish(self):
        for far in (1, 2):
            pl.when(self.has(self.step * far))(lambda far=far: self.group_copy(far).wait_send())
        for copy in self.out_copies + self.back_copies + self.relay_copies:
            copy.wait_send()


FAR, NEAR = (3, 5), (2, 6, 1, 7)
DIRECT = FAR + NEAR
HEADS_BUF = pltpu.VMEM((HEADS, WIDTH, WIDTH), f32)
SCAN_SCRATCH = [
    HEADS_BUF, HEADS_BUF, pltpu.VMEM((WIDTH, WIDTH), f32), pltpu.VMEM((2, WIDTH, WIDTH), f32),
    pltpu.VMEM((4, HALF, WIDTH), f32),
] + [pltpu.SemaphoreType.DMA((NY,))] * 4 + [pltpu.SemaphoreType.DMA((4,))] * 4 + [pltpu.SemaphoreType.DMA((2,))] * 2


def attention_block(q_ref, k_ref, v_ref, rate_ref, len_ref, attention_buf):
    base = lax.axis_index("ctx") * ROWS
    same, distance = pair_tables(base, doc_bounds(len_ref))
    for h in range(HEADS):
        cols = pl.ds(h * WIDTH, WIDTH)
        v = v_ref[:, cols]
        mask = jnp.where(same, jnp.exp(-rate_ref[h] * distance), 0.0)
        s_high, s_low = split(matmul(q_ref[:, cols], k_ref[:, cols], NT) * mask)
        attention_buf[:, cols] = matmul(s_high, v, NN) + matmul(s_low, v, NN)


def head_columns(head):
    return pl.ds(pl.multiple_of(head * WIDTH, WIDTH), WIDTH)


def attention_head(q_ref, rate_ref, tables, in_ref, attention_buf, head):
    offsets, entering, _ = tables
    cols = head_columns(head)
    q = q_ref[:, cols]
    entry = jnp.where(entering, jnp.exp(-rate_ref[head] * offsets), 0.0)
    in_high, in_low = split(in_ref[head])
    attention_buf[:, cols] += entry * (matmul(q, in_high, NN) + matmul(q, in_low, NN))


def norm_part(gain_ref, attention_buf, normed_buf):
    attention = attention_buf[...]
    mean = jnp.mean(attention * attention, axis=-1, keepdims=True)
    normed_buf[...] = (attention * lax.rsqrt(mean + norm_eps) * gain_ref[...]).astype(bf16)


def gradient_head(k_ref, v_ref, rate_ref, tables, grad_ref, dk_part, dv_part, dk_ref, dv_ref, head):
    offsets, _, leaving = tables
    cols = head_columns(head)
    k, v = k_ref[:, cols], v_ref[:, cols]
    leave = jnp.where(leaving, jnp.exp(-rate_ref[head] * (ROWS - offsets)), 0.0)
    grad_high, grad_low = split(grad_ref[head])
    dk = leave * (matmul(v, grad_high, NT) + matmul(v, grad_low, NT))
    dk_ref[:, cols] = (dk_part[:, cols] + dk).astype(bf16)
    dv = leave * (matmul(k, grad_high, NN) + matmul(k, grad_low, NN))
    dv_ref[:, cols] = (dv_part[:, cols] + dv).astype(bf16)


def hand_over(*refs):
    for src, dst in zip(refs[:len(refs) // 2], refs[len(refs) // 2:]):
        dst[...] = src[...]


def pair_tables(base, bounds):
    rows = lax.broadcasted_iota(jnp.int32, (ROWS, ROWS), 0)
    columns = lax.broadcasted_iota(jnp.int32, (ROWS, ROWS), 1)
    same = (doc_of(base + rows, bounds) == doc_of(base + columns, bounds)) & (rows >= columns)
    return same, jnp.maximum(rows - columns, 0).astype(f32)


def block_part(q_ref, k_ref, v_ref, g_ref, rate_ref, len_ref, in_ref, dq_ref, dk_ref, dv_ref):
    base = lax.axis_index("ctx") * ROWS
    bounds = doc_bounds(len_ref)
    offsets, entering, _ = edge_tables(base, bounds)
    same, distance = pair_tables(base, bounds)
    for h in range(HEADS):
        cols = pl.ds(h * WIDTH, WIDTH)
        rate = rate_ref[h]
        q, k, v, g = q_ref[:, cols], k_ref[:, cols], v_ref[:, cols], g_ref[:, cols]
        mask = jnp.where(same, jnp.exp(-rate * distance), 0.0)
        entry = jnp.where(entering, jnp.exp(-rate * offsets), 0.0)
        s_high, s_low = split(matmul(q, k, NT) * mask)
        d_high, d_low = split(matmul(g, v, NT) * mask)
        in_high, in_low = split(in_ref[h])
        dq = matmul(d_high, k, NN) + matmul(d_low, k, NN)
        dq += entry * (matmul(g, in_high, NT) + matmul(g, in_low, NT))
        dq_ref[:, cols] = dq.astype(bf16)
        dk_ref[:, cols] = matmul(d_high, q, TN) + matmul(d_low, q, TN)
        dv_ref[:, cols] = matmul(s_high, g, TN) + matmul(s_low, g, TN)


def main_kernel(
    scale, q_ref, k_ref, v_ref, g_ref, layer_ref, gain_ref, rate_ref, len_ref,
    dq_ref, dk_ref, dv_ref, out_ref,
    grad_ref, dk_part, dv_part, state_ref, pull_ref, carry_ref, in_ref, px_ref, pz_ref, attention_buf, normed_buf, cx_buf, ax_buf, x_buf, bx_buf, xz_buf, cz_buf, az_buf, z_buf, bz_buf, zx_buf, c_buf, y_buf,
    core_send, core_recv, x_send, x_recv, xz_send, xz_recv,
    z_send, z_recv, zx_send, zx_recv, y_send, y_recv, *scratch,
):
    dp, ctx, z_low, y = place()
    x, z_high, core = dp // 4, lax.rem(dp // 2, 2), lax.rem(dp, 2)
    z = z_high * 4 + z_low
    twin = (dp + 1 - 2 * core, ctx)

    def at_x(k):
        return (lax.rem(x + k, NX) * 4 + lax.rem(dp, 4), ctx)

    def at_z(k):
        there = lax.rem(z + k, NZ)
        return (x * 4 + there // 4 * 2 + core, lax.rem(there, 4) * NY + y)

    def at_y(k):
        return (dp, ctx - y + lax.rem(y + k, NY))

    ahead = Scan(1, state_ref, carry_ref, in_ref, scratch[:15])
    scan = Scan(-1, pull_ref, carry_ref, grad_ref, scratch[15:])
    partners = (
        [twin] + [at_x(k) for k in range(1, NX)] + [at_z(k) for k in range(1, NZ)]
        + [at_y(k) for k in range(1, NY)]
    )
    barrier = pltpu.get_barrier_semaphore()
    for device in partners:
        pl.semaphore_signal(barrier, inc=1, device_id=device, device_id_type=MESH)
    state_part(k_ref, v_ref, rate_ref, len_ref, state_ref, carry_ref)
    pl.semaphore_wait(barrier, len(partners))
    ahead.half_way(0)
    ahead.scatter(DIRECT)
    pull_part(q_ref, g_ref, rate_ref, len_ref, pull_ref)
    ahead.pass_on(0)
    attention_block(q_ref, k_ref, v_ref, rate_ref, len_ref, attention_buf)
    ahead.totals()
    scan.half_way(0)
    scan.scatter(NEAR)
    ahead.combine()
    ahead.half_way(1)
    ahead.give_back(DIRECT)
    scan.pass_on(0)
    ahead.pass_on(1)
    scan.scatter(FAR)
    tables = edge_tables(ctx * ROWS, doc_bounds(len_ref))
    ahead.arrive(
        functools.partial(attention_head, q_ref, rate_ref, tables, in_ref, attention_buf)
    )
    norm_part(gain_ref, attention_buf, normed_buf)

    def product(block, columns):
        return matmul(normed_buf[:, head_columns(block)], layer_ref[:, columns], TN)

    for h in range(HEADS):
        rows = product(h, slice(XCOLS, None))
        for half in range(2):
            for low in range(NZL):
                row = half * 64 + low * 16
                pz_ref[h % 2 * 4 + low, half, h // 2] = rows[row:row + 16]
    core_sems = (core_send, core_recv)
    core_copies = started([send(pz_ref.at[:, 1 - core], cz_buf, core_sems, NX, twin)])

    def to_twin(k):
        there = lax.rem(x + k, NX)
        for high in range(2):
            rows = product(there * 2 + high, slice(0, XCOLS))
            for half in range(2):
                px_ref[there, high, half] = rows[half * 64:half * 64 + 64]
        core_copies.extend(
            started([send(px_ref.at[there, :, 1 - core], cx_buf.at[k], core_sems, k, twin)])
        )

    def to_z(offsets):
        return started([
            send(az_buf.at[lax.rem(z + k, NZ)], z_buf.at[k], (z_send, z_recv), k, at_z(k))
            for k in offsets
        ])

    order = tuple(range(1, NX)) + (0,)
    for k in order[:2]:
        to_twin(k)
    core_copies[0].wait_recv()
    az_buf[...] = pz_ref[:, core] + cz_buf[...]
    z_copies = to_z((3, 4, 5))
    for k in order[2:]:
        to_twin(k)
    x_copies = []
    for k, copy in zip(order, core_copies[1:]):
        copy.wait_recv()
        ax_buf[k] = px_ref[lax.rem(x + k, NX), :, core] + cx_buf[k]
        if k:
            x_copies += started([send(ax_buf.at[k], x_buf.at[k], (x_send, x_recv), k, at_x(k))])
    scan.totals()
    z_copies = to_z((1, 2)) + z_copies + to_z((6, 7))
    block_part(q_ref, k_ref, v_ref, g_ref, rate_ref, len_ref, in_ref, dq_ref, dk_part, dv_part)
    scan.combine()
    scan.half_way(1)
    scan.give_back(DIRECT)

    def gather(total, copies, buf):
        for k, copy in enumerate(copies, 1):
            copy.wait_recv()
            total = total + buf[k]
        return total

    bx_buf[...] = gather(ax_buf[0], x_copies, x_buf).reshape(bx_buf.shape)
    xz_copies = started([
        send(bx_buf.at[lax.rem(z + k, NZ)], xz_buf.at[k], (xz_send, xz_recv), k, at_z(k))
        for k in range(1, NZ)
    ])
    scan.pass_on(1)
    bz_buf[...] = gather(az_buf[z], z_copies, z_buf)
    zx_copies = started([
        send(bz_buf.at[lax.rem(x + k, NX)], zx_buf.at[k], (zx_send, zx_recv), k, at_x(k))
        for k in range(1, NX)
    ])
    right = gather(bz_buf[x], zx_copies, zx_buf)
    left = gather(bx_buf[z], xz_copies, xz_buf)
    for j in range(NY):
        c_buf[j, :, :XCOLS] = left[2 * j:2 * j + 2, :]
        c_buf[j, :, XCOLS:] = right[2 * j:2 * j + 2, :]
    y_copies = started([
        send(c_buf.at[lax.rem(y + k, NY)], y_buf.at[k], (y_send, y_recv), k, at_y(k))
        for k in range(1, NY)
    ])
    scan.arrive(functools.partial(
        gradient_head, k_ref, v_ref, rate_ref, tables, grad_ref, dk_part, dv_part, dk_ref, dv_ref
    ))
    out_ref[...] = gather(c_buf[y], y_copies, y_buf) * scale
    scan.finish()
    ahead.finish()
    for copy in core_copies + x_copies + z_copies + xz_copies + zx_copies + y_copies:
        copy.wait_send()


def on_device(queries, keys, values, out_grad, layer_grad, norm_gain, decay_rates, doc_lengths):
    rows, features, bucket = ROWS, HEADS * WIDTH, layer_grad.shape[2]
    scale = 1.0 / math.sqrt(rows * lax.axis_size("dp") * lax.axis_size("ctx"))
    q, k, v, g = (a.reshape(rows, features) for a in (queries, keys, values, out_grad))
    layer = layer_grad.reshape(rows, bucket)
    zcols = bucket - XCOLS
    dma = pltpu.SemaphoreType.DMA
    grad_shape = jax.ShapeDtypeStruct((rows, features), bf16)
    results = (grad_shape,) * 3 + (jax.ShapeDtypeStruct((2, bucket), f32),)
    parts = pl.pallas_call(
        functools.partial(main_kernel, scale),
        out_shape=results,
        in_specs=[VMEM_SPEC] * 6 + [SMEM_SPEC] * 2,
        out_specs=(VMEM_SPEC,) * 4,
        scratch_shapes=[
            HEADS_BUF,
            pltpu.VMEM((rows, features), f32),
            pltpu.VMEM((rows, features), f32),
            HEADS_BUF,
            HEADS_BUF,
            pltpu.VMEM((16, WIDTH), f32),
            HEADS_BUF,
            pltpu.VMEM((NX, 2, 2, 64, XCOLS), f32),
            pltpu.VMEM((NZ, 2, NX, 16, zcols), f32),
            pltpu.VMEM((rows, features), f32),
            pltpu.VMEM((rows, features), bf16),
        ]
        + [pltpu.VMEM((NX, 2, 64, XCOLS), f32)] * 3
        + [pltpu.VMEM((NZ, 16, XCOLS), f32)] * 2
        + [pltpu.VMEM((NZ, NX, 16, zcols), f32)] * 3
        + [pltpu.VMEM((NX, 16, zcols), f32)] * 2
        + [pltpu.VMEM((NY, 2, bucket), f32)] * 2
        + [dma((NX + 1,))] * 2 + [dma((NX,))] * 2 + [dma((NZ,))] * 4
        + [dma((NX,))] * 2 + [dma((NY,))] * 2
        + SCAN_SCRATCH * 2,
        compiler_params=pltpu.CompilerParams(collective_id=0, has_side_effects=True),
        name="main",
    )(q, k, v, g, layer, norm_gain.reshape(1, features), decay_rates, doc_lengths)
    query_grad, key_grad, value_grad, proj_grad = pl.pallas_call(
        hand_over,
        out_shape=results,
        in_specs=[VMEM_SPEC] * 4,
        out_specs=(VMEM_SPEC,) * 4,
        name="results",
    )(*parts)
    shape_out = (1, rows, features)
    return (
        query_grad.reshape(shape_out),
        key_grad.reshape(shape_out),
        value_grad.reshape(shape_out),
        proj_grad,
    )


def solution(mesh):
    block = P("dp", "ctx", None)
    return jax.shard_map(
        on_device,
        mesh=mesh,
        in_specs=(block,) * 5 + (P(), P(), P("dp", None)),
        out_specs=(block,) * 3 + (P(("dp", "ctx"), None),),
        check_vma=False,
    )
```

```python
import functools
import math

import jax
import jax.numpy as jnp
from jax import lax
from jax.experimental import pallas as pl
from jax.experimental.pallas import tpu as pltpu
from jax.sharding import PartitionSpec as P

norm_eps = 1e-06
HEADS, WIDTH, ROWS = 8, 128, 128
NX, NZ, NY, NZL = 4, 8, 8, 4
XCOLS = 512
MESH = pl.DeviceIdType.MESH
f32, bf16 = jnp.float32, jnp.bfloat16
VMEM_SPEC = pl.BlockSpec(memory_space=pltpu.VMEM)
SMEM_SPEC = pl.BlockSpec(memory_space=pltpu.SMEM)


def split(value):
    high = value.astype(bf16)
    return high, (value - high.astype(f32)).astype(bf16)


def matmul(a, b, dims):
    return lax.dot_general(a, b, (dims, ((), ())), preferred_element_type=f32)


NN, NT, TN = ((1,), (0,)), ((1,), (1,)), ((0,), (0,))


def doc_bounds(len_ref):
    first = len_ref[0, 0]
    second = first + len_ref[0, 1]
    return first, second, second + len_ref[0, 2]


def doc_of(positions, bounds):
    return sum((positions >= bound).astype(jnp.int32) for bound in bounds)


def doc_of_scalar(position, bounds):
    return sum(jnp.where(position >= bound, 1, 0) for bound in bounds)


def edge_tables(base, bounds):
    offsets = lax.broadcasted_iota(jnp.int32, (ROWS, WIDTH), 0)
    docs = doc_of(base + offsets, bounds)
    entering = docs == doc_of_scalar(base - 1, bounds)
    leaving = docs == doc_of_scalar(base + ROWS - 1, bounds)
    return offsets.astype(f32), entering, leaving


def state_part(k_ref, v_ref, rate_ref, len_ref, state_ref, carry_ref):
    ctx = lax.axis_index("ctx")
    bounds = doc_bounds(len_ref)
    offsets, _, leaving = edge_tables(ctx * ROWS, bounds)
    for h in range(HEADS):
        cols = pl.ds(h * WIDTH, WIDTH)
        leave = jnp.where(leaving, jnp.exp(-rate_ref[h] * (ROWS - offsets)), 0.0)
        high, low = split(k_ref[:, cols].astype(f32) * leave)
        v = v_ref[:, cols]
        state_ref[h] = matmul(high, v, TN) + matmul(low, v, TN)
    group, own = ctx // NY, lax.rem(ctx, NY)
    rate = rate_ref[own]

    def carry(first, blocks):
        start = first * ROWS
        whole = doc_of_scalar(start - 1, bounds) == doc_of_scalar(start + blocks * ROWS - 1, bounds)
        decay = jnp.exp(jnp.full((1, WIDTH), -rate * float(blocks * ROWS), f32))
        return jnp.where(whole, decay, 0.0)

    for j in range(NY):
        carry_ref[pl.ds(j, 1), :] = carry(group * NY + j, 1)
    carry_ref[pl.ds(8, 1), :] = carry((group - 1) * NY, NY)
    carry_ref[pl.ds(9, 1), :] = carry((group + 1) * NY, NY)


def pull_part(q_ref, g_ref, rate_ref, len_ref, pull_ref):
    offsets, entering, _ = edge_tables(lax.axis_index("ctx") * ROWS, doc_bounds(len_ref))
    for h in range(HEADS):
        cols = pl.ds(h * WIDTH, WIDTH)
        entry = jnp.where(entering, jnp.exp(-rate_ref[h] * offsets), 0.0)
        high, low = split(q_ref[:, cols].astype(f32) * entry)
        g = g_ref[:, cols]
        pull_ref[h] = matmul(high, g, TN) + matmul(low, g, TN)


def place():
    dp, ctx = lax.axis_index("dp"), lax.axis_index("ctx")
    return dp, ctx, ctx // NY, lax.rem(ctx, NY)


def send(src, dst, sems, at, device):
    return pltpu.make_async_remote_copy(
        src_ref=src, dst_ref=dst, send_sem=sems[0].at[at], recv_sem=sems[1].at[at],
        device_id=device, device_id_type=MESH,
    )


def started(copies):
    for copy in copies:
        copy.start()
    return copies


class Scan:
    def __init__(self, step, src, carry, result, scratch):
        self.step, self.src, self.carry_ref, self.result = step, src, carry, result
        self.buf, self.back, self.total, self.group = scratch[:4]
        self.out_sems, self.back_sems, self.group_sems = scratch[4:6], scratch[6:8], scratch[8:10]
        self.dp, _, self.z, self.y = place()
        self.out_copies, self.back_copies = [], []
        self.order = range(NY) if step > 0 else range(NY - 1, -1, -1)

    def around(self, k):
        return lax.rem(self.y + k, NY)

    def at_y(self, k):
        return (self.dp, self.z * NY + self.around(k))

    def carry(self, j):
        return self.carry_ref[pl.ds(j, 1), :]

    def block(self, j):
        return self.buf[lax.rem(self.y - j + NY, NY)]

    def scatter(self, offsets):
        self.out_copies += started([
            send(self.src.at[self.around(k)], self.buf.at[k], self.out_sems, k, self.at_y(k))
            for k in offsets
        ])

    def group_copy(self, far):
        there = (self.dp, (self.z + self.step * far) * NY + self.y)
        return send(self.total, self.group.at[far - 1], self.group_sems, far - 1, there)

    def has(self, far):
        other = self.z + far
        return (other >= 0) & (other < NZL)

    def totals(self):
        self.buf[0] = self.src[self.y]
        for copy in self.out_copies:
            copy.wait_recv()
        total = jnp.zeros((WIDTH, WIDTH), f32)
        for j in self.order:
            total = self.carry(j) * total + self.block(j)
        self.total[...] = total
        for far in (1, 2):
            pl.when(self.has(self.step * far))(lambda far=far: self.group_copy(far).start())

    def combine(self):
        for far in (1, 2):
            source = self.has(-self.step * far)
            pl.when(source)(lambda far=far: self.group_copy(far).wait_recv())

            @pl.when(jnp.logical_not(source))
            def _():
                self.group[far - 1] = jnp.zeros((WIDTH, WIDTH), f32)

        now = self.group[0] + self.carry(8 if self.step > 0 else 9) * self.group[1]
        for j in self.order:
            self.back[j] = now
            now = self.carry(j) * now + self.block(j)

    def give_back(self, offsets):
        self.back_copies += started([
            send(self.back.at[self.around(k)], self.result.at[self.y], self.back_sems, k, self.at_y(k))
            for k in offsets
        ])

    def arrive(self, use):
        self.result[self.y] = self.back[self.y]
        use(self.y)
        for k in DIRECT:
            send(
                self.back.at[0], self.result.at[self.around(NY - k)], self.back_sems, k, self.at_y(k)
            ).wait_recv()
            use(self.around(NY - k))

    def finish(self):
        for far in (1, 2):
            pl.when(self.has(self.step * far))(lambda far=far: self.group_copy(far).wait_send())
        for copy in self.out_copies + self.back_copies:
            copy.wait_send()


FAR, NEAR = (4, 3, 5), (2, 6, 1, 7)
DIRECT = FAR + NEAR
HEADS_BUF = pltpu.VMEM((HEADS, WIDTH, WIDTH), f32)
SCAN_SCRATCH = [
    HEADS_BUF, HEADS_BUF, pltpu.VMEM((WIDTH, WIDTH), f32), pltpu.VMEM((2, WIDTH, WIDTH), f32),
] + [pltpu.SemaphoreType.DMA((NY,))] * 4 + [pltpu.SemaphoreType.DMA((2,))] * 2


def attention_block(q_ref, k_ref, v_ref, rate_ref, len_ref, attention_buf):
    base = lax.axis_index("ctx") * ROWS
    same, distance = pair_tables(base, doc_bounds(len_ref))
    for h in range(HEADS):
        cols = pl.ds(h * WIDTH, WIDTH)
        v = v_ref[:, cols]
        mask = jnp.where(same, jnp.exp(-rate_ref[h] * distance), 0.0)
        s_high, s_low = split(matmul(q_ref[:, cols], k_ref[:, cols], NT) * mask)
        attention_buf[:, cols] = matmul(s_high, v, NN) + matmul(s_low, v, NN)


def head_columns(head):
    return pl.ds(pl.multiple_of(head * WIDTH, WIDTH), WIDTH)


def attention_head(q_ref, rate_ref, tables, in_ref, attention_buf, head):
    offsets, entering, _ = tables
    cols = head_columns(head)
    q = q_ref[:, cols]
    entry = jnp.where(entering, jnp.exp(-rate_ref[head] * offsets), 0.0)
    in_high, in_low = split(in_ref[head])
    attention_buf[:, cols] += entry * (matmul(q, in_high, NN) + matmul(q, in_low, NN))


def norm_part(gain_ref, attention_buf, normed_buf):
    attention = attention_buf[...]
    mean = jnp.mean(attention * attention, axis=-1, keepdims=True)
    normed_buf[...] = (attention * lax.rsqrt(mean + norm_eps) * gain_ref[...]).astype(bf16)


def gradient_head(k_ref, v_ref, rate_ref, tables, grad_ref, dk_part, dv_part, dk_ref, dv_ref, head):
    offsets, _, leaving = tables
    cols = head_columns(head)
    k, v = k_ref[:, cols], v_ref[:, cols]
    leave = jnp.where(leaving, jnp.exp(-rate_ref[head] * (ROWS - offsets)), 0.0)
    grad_high, grad_low = split(grad_ref[head])
    dk = leave * (matmul(v, grad_high, NT) + matmul(v, grad_low, NT))
    dk_ref[:, cols] = (dk_part[:, cols] + dk).astype(bf16)
    dv = leave * (matmul(k, grad_high, NN) + matmul(k, grad_low, NN))
    dv_ref[:, cols] = (dv_part[:, cols] + dv).astype(bf16)


def hand_over(*refs):
    for src, dst in zip(refs[:len(refs) // 2], refs[len(refs) // 2:]):
        dst[...] = src[...]


def pair_tables(base, bounds):
    rows = lax.broadcasted_iota(jnp.int32, (ROWS, ROWS), 0)
    columns = lax.broadcasted_iota(jnp.int32, (ROWS, ROWS), 1)
    same = (doc_of(base + rows, bounds) == doc_of(base + columns, bounds)) & (rows >= columns)
    return same, jnp.maximum(rows - columns, 0).astype(f32)


def block_part(q_ref, k_ref, v_ref, g_ref, rate_ref, len_ref, in_ref, dq_ref, dk_ref, dv_ref):
    base = lax.axis_index("ctx") * ROWS
    bounds = doc_bounds(len_ref)
    offsets, entering, _ = edge_tables(base, bounds)
    same, distance = pair_tables(base, bounds)
    for h in range(HEADS):
        cols = pl.ds(h * WIDTH, WIDTH)
        rate = rate_ref[h]
        q, k, v, g = q_ref[:, cols], k_ref[:, cols], v_ref[:, cols], g_ref[:, cols]
        mask = jnp.where(same, jnp.exp(-rate * distance), 0.0)
        entry = jnp.where(entering, jnp.exp(-rate * offsets), 0.0)
        s_high, s_low = split(matmul(q, k, NT) * mask)
        d_high, d_low = split(matmul(g, v, NT) * mask)
        in_high, in_low = split(in_ref[h])
        dq = matmul(d_high, k, NN) + matmul(d_low, k, NN)
        dq += entry * (matmul(g, in_high, NT) + matmul(g, in_low, NT))
        dq_ref[:, cols] = dq.astype(bf16)
        dk_ref[:, cols] = matmul(d_high, q, TN) + matmul(d_low, q, TN)
        dv_ref[:, cols] = matmul(s_high, g, TN) + matmul(s_low, g, TN)


def main_kernel(
    scale, q_ref, k_ref, v_ref, g_ref, layer_ref, gain_ref, rate_ref, len_ref,
    dq_ref, dk_ref, dv_ref, out_ref,
    grad_ref, dk_part, dv_part, state_ref, pull_ref, carry_ref, in_ref, px_ref, pz_ref, attention_buf, normed_buf, cx_buf, ax_buf, x_buf, bx_buf, xz_buf, cz_buf, az_buf, z_buf, bz_buf, zx_buf, c_buf, y_buf,
    core_send, core_recv, x_send, x_recv, xz_send, xz_recv,
    z_send, z_recv, zx_send, zx_recv, y_send, y_recv, *scratch,
):
    dp, ctx, z_low, y = place()
    x, z_high, core = dp // 4, lax.rem(dp // 2, 2), lax.rem(dp, 2)
    z = z_high * 4 + z_low
    twin = (dp + 1 - 2 * core, ctx)

    def at_x(k):
        return (lax.rem(x + k, NX) * 4 + lax.rem(dp, 4), ctx)

    def at_z(k):
        there = lax.rem(z + k, NZ)
        return (x * 4 + there // 4 * 2 + core, lax.rem(there, 4) * NY + y)

    def at_y(k):
        return (dp, ctx - y + lax.rem(y + k, NY))

    ahead = Scan(1, state_ref, carry_ref, in_ref, scratch[:10])
    scan = Scan(-1, pull_ref, carry_ref, grad_ref, scratch[10:])
    partners = (
        [twin] + [at_x(k) for k in range(1, NX)] + [at_z(k) for k in range(1, NZ)]
        + [at_y(k) for k in range(1, NY)]
    )
    barrier = pltpu.get_barrier_semaphore()
    for device in partners:
        pl.semaphore_signal(barrier, inc=1, device_id=device, device_id_type=MESH)
    state_part(k_ref, v_ref, rate_ref, len_ref, state_ref, carry_ref)
    pl.semaphore_wait(barrier, len(partners))
    ahead.scatter(DIRECT)
    pull_part(q_ref, g_ref, rate_ref, len_ref, pull_ref)
    attention_block(q_ref, k_ref, v_ref, rate_ref, len_ref, attention_buf)
    ahead.totals()
    scan.scatter(NEAR)
    ahead.combine()
    ahead.give_back(DIRECT)
    scan.scatter(FAR)
    tables = edge_tables(ctx * ROWS, doc_bounds(len_ref))
    ahead.arrive(
        functools.partial(attention_head, q_ref, rate_ref, tables, in_ref, attention_buf)
    )
    norm_part(gain_ref, attention_buf, normed_buf)

    def product(block, columns):
        return matmul(normed_buf[:, head_columns(block)], layer_ref[:, columns], TN)

    for h in range(HEADS):
        rows = product(h, slice(XCOLS, None))
        for half in range(2):
            for low in range(NZL):
                row = half * 64 + low * 16
                pz_ref[h % 2 * 4 + low, half, h // 2] = rows[row:row + 16]
    core_sems = (core_send, core_recv)
    core_copies = started([send(pz_ref.at[:, 1 - core], cz_buf, core_sems, NX, twin)])

    def to_twin(k):
        there = lax.rem(x + k, NX)
        for high in range(2):
            rows = product(there * 2 + high, slice(0, XCOLS))
            for half in range(2):
                px_ref[there, high, half] = rows[half * 64:half * 64 + 64]
        core_copies.extend(
            started([send(px_ref.at[there, :, 1 - core], cx_buf.at[k], core_sems, k, twin)])
        )

    def to_z(offsets):
        return started([
            send(az_buf.at[lax.rem(z + k, NZ)], z_buf.at[k], (z_send, z_recv), k, at_z(k))
            for k in offsets
        ])

    order = tuple(range(1, NX)) + (0,)
    for k in order[:2]:
        to_twin(k)
    core_copies[0].wait_recv()
    az_buf[...] = pz_ref[:, core] + cz_buf[...]
    z_copies = to_z((3, 4, 5))
    for k in order[2:]:
        to_twin(k)
    x_copies = []
    for k, copy in zip(order, core_copies[1:]):
        copy.wait_recv()
        ax_buf[k] = px_ref[lax.rem(x + k, NX), :, core] + cx_buf[k]
        if k:
            x_copies += started([send(ax_buf.at[k], x_buf.at[k], (x_send, x_recv), k, at_x(k))])
    scan.totals()
    z_copies = to_z((1, 2)) + z_copies + to_z((6, 7))
    block_part(q_ref, k_ref, v_ref, g_ref, rate_ref, len_ref, in_ref, dq_ref, dk_part, dv_part)
    scan.combine()
    scan.give_back(DIRECT)

    def gather(total, copies, buf):
        for k, copy in enumerate(copies, 1):
            copy.wait_recv()
            total = total + buf[k]
        return total

    bx_buf[...] = gather(ax_buf[0], x_copies, x_buf).reshape(bx_buf.shape)
    xz_copies = started([
        send(bx_buf.at[lax.rem(z + k, NZ)], xz_buf.at[k], (xz_send, xz_recv), k, at_z(k))
        for k in range(1, NZ)
    ])
    bz_buf[...] = gather(az_buf[z], z_copies, z_buf)
    zx_copies = started([
        send(bz_buf.at[lax.rem(x + k, NX)], zx_buf.at[k], (zx_send, zx_recv), k, at_x(k))
        for k in range(1, NX)
    ])
    right = gather(bz_buf[x], zx_copies, zx_buf)
    left = gather(bx_buf[z], xz_copies, xz_buf)
    for j in range(NY):
        c_buf[j, :, :XCOLS] = left[2 * j:2 * j + 2, :]
        c_buf[j, :, XCOLS:] = right[2 * j:2 * j + 2, :]
    y_copies = started([
        send(c_buf.at[lax.rem(y + k, NY)], y_buf.at[k], (y_send, y_recv), k, at_y(k))
        for k in range(1, NY)
    ])
    scan.arrive(functools.partial(
        gradient_head, k_ref, v_ref, rate_ref, tables, grad_ref, dk_part, dv_part, dk_ref, dv_ref
    ))
    out_ref[...] = gather(c_buf[y], y_copies, y_buf) * scale
    scan.finish()
    ahead.finish()
    for copy in core_copies + x_copies + z_copies + xz_copies + zx_copies + y_copies:
        copy.wait_send()


def on_device(queries, keys, values, out_grad, layer_grad, norm_gain, decay_rates, doc_lengths):
    rows, features, bucket = ROWS, HEADS * WIDTH, layer_grad.shape[2]
    scale = 1.0 / math.sqrt(rows * lax.axis_size("dp") * lax.axis_size("ctx"))
    q, k, v, g = (a.reshape(rows, features) for a in (queries, keys, values, out_grad))
    layer = layer_grad.reshape(rows, bucket)
    zcols = bucket - XCOLS
    dma = pltpu.SemaphoreType.DMA
    grad_shape = jax.ShapeDtypeStruct((rows, features), bf16)
    results = (grad_shape,) * 3 + (jax.ShapeDtypeStruct((2, bucket), f32),)
    parts = pl.pallas_call(
        functools.partial(main_kernel, scale),
        out_shape=results,
        in_specs=[VMEM_SPEC] * 6 + [SMEM_SPEC] * 2,
        out_specs=(VMEM_SPEC,) * 4,
        scratch_shapes=[
            HEADS_BUF,
            pltpu.VMEM((rows, features), f32),
            pltpu.VMEM((rows, features), f32),
            HEADS_BUF,
            HEADS_BUF,
            pltpu.VMEM((16, WIDTH), f32),
            HEADS_BUF,
            pltpu.VMEM((NX, 2, 2, 64, XCOLS), f32),
            pltpu.VMEM((NZ, 2, NX, 16, zcols), f32),
            pltpu.VMEM((rows, features), f32),
            pltpu.VMEM((rows, features), bf16),
        ]
        + [pltpu.VMEM((NX, 2, 64, XCOLS), f32)] * 3
        + [pltpu.VMEM((NZ, 16, XCOLS), f32)] * 2
        + [pltpu.VMEM((NZ, NX, 16, zcols), f32)] * 3
        + [pltpu.VMEM((NX, 16, zcols), f32)] * 2
        + [pltpu.VMEM((NY, 2, bucket), f32)] * 2
        + [dma((NX + 1,))] * 2 + [dma((NX,))] * 2 + [dma((NZ,))] * 4
        + [dma((NX,))] * 2 + [dma((NY,))] * 2
        + SCAN_SCRATCH * 2,
        compiler_params=pltpu.CompilerParams(collective_id=0, has_side_effects=True),
        name="main",
    )(q, k, v, g, layer, norm_gain.reshape(1, features), decay_rates, doc_lengths)
    query_grad, key_grad, value_grad, proj_grad = pl.pallas_call(
        hand_over,
        out_shape=results,
        in_specs=[VMEM_SPEC] * 4,
        out_specs=(VMEM_SPEC,) * 4,
        name="results",
    )(*parts)
    shape_out = (1, rows, features)
    return (
        query_grad.reshape(shape_out),
        key_grad.reshape(shape_out),
        value_grad.reshape(shape_out),
        proj_grad,
    )


def solution(mesh):
    block = P("dp", "ctx", None)
    return jax.shard_map(
        on_device,
        mesh=mesh,
        in_specs=(block,) * 5 + (P(), P(), P("dp", None)),
        out_specs=(block,) * 3 + (P(("dp", "ctx"), None),),
        check_vma=False,
    )
```

```python
import functools
import math

import jax
import jax.numpy as jnp
from jax import lax
from jax.experimental import pallas as pl
from jax.experimental.pallas import tpu as pltpu
from jax.sharding import PartitionSpec as P

norm_eps = 1e-06
HEADS, WIDTH, ROWS = 8, 128, 128
NX, NZ, NY, NZL = 4, 8, 8, 4
XCOLS = 512
MESH = pl.DeviceIdType.MESH
f32, bf16 = jnp.float32, jnp.bfloat16
VMEM_SPEC = pl.BlockSpec(memory_space=pltpu.VMEM)
SMEM_SPEC = pl.BlockSpec(memory_space=pltpu.SMEM)


def split(value):
    high = value.astype(bf16)
    return high, (value - high.astype(f32)).astype(bf16)


def matmul(a, b, dims):
    return lax.dot_general(a, b, (dims, ((), ())), preferred_element_type=f32)


NN, NT, TN = ((1,), (0,)), ((1,), (1,)), ((0,), (0,))


def doc_bounds(len_ref):
    first = len_ref[0, 0]
    second = first + len_ref[0, 1]
    return first, second, second + len_ref[0, 2]


def doc_of(positions, bounds):
    return sum((positions >= bound).astype(jnp.int32) for bound in bounds)


def doc_of_scalar(position, bounds):
    return sum(jnp.where(position >= bound, 1, 0) for bound in bounds)


def edge_tables(base, bounds):
    offsets = lax.broadcasted_iota(jnp.int32, (ROWS, WIDTH), 0)
    docs = doc_of(base + offsets, bounds)
    entering = docs == doc_of_scalar(base - 1, bounds)
    leaving = docs == doc_of_scalar(base + ROWS - 1, bounds)
    return offsets.astype(f32), entering, leaving


def state_part(k_ref, v_ref, rate_ref, len_ref, state_ref, carry_ref):
    ctx = lax.axis_index("ctx")
    bounds = doc_bounds(len_ref)
    offsets, _, leaving = edge_tables(ctx * ROWS, bounds)
    for h in range(HEADS):
        cols = pl.ds(h * WIDTH, WIDTH)
        leave = jnp.where(leaving, jnp.exp(-rate_ref[h] * (ROWS - offsets)), 0.0)
        high, low = split(k_ref[:, cols].astype(f32) * leave)
        v = v_ref[:, cols]
        state_ref[h] = matmul(high, v, TN) + matmul(low, v, TN)
    group, own = ctx // NY, lax.rem(ctx, NY)
    rate = rate_ref[own]

    def carry(first, blocks):
        start = first * ROWS
        whole = doc_of_scalar(start - 1, bounds) == doc_of_scalar(start + blocks * ROWS - 1, bounds)
        decay = jnp.exp(jnp.full((1, WIDTH), -rate * float(blocks * ROWS), f32))
        return jnp.where(whole, decay, 0.0)

    for j in range(NY):
        carry_ref[pl.ds(j, 1), :] = carry(group * NY + j, 1)
    carry_ref[pl.ds(8, 1), :] = carry((group - 1) * NY, NY)
    carry_ref[pl.ds(9, 1), :] = carry((group + 1) * NY, NY)


def pull_part(q_ref, g_ref, rate_ref, len_ref, pull_ref):
    offsets, entering, _ = edge_tables(lax.axis_index("ctx") * ROWS, doc_bounds(len_ref))
    for h in range(HEADS):
        cols = pl.ds(h * WIDTH, WIDTH)
        entry = jnp.where(entering, jnp.exp(-rate_ref[h] * offsets), 0.0)
        high, low = split(q_ref[:, cols].astype(f32) * entry)
        g = g_ref[:, cols]
        pull_ref[h] = matmul(high, g, TN) + matmul(low, g, TN)


def place():
    dp, ctx = lax.axis_index("dp"), lax.axis_index("ctx")
    return dp, ctx, ctx // NY, lax.rem(ctx, NY)


def send(src, dst, sems, at, device):
    return pltpu.make_async_remote_copy(
        src_ref=src, dst_ref=dst, send_sem=sems[0].at[at], recv_sem=sems[1].at[at],
        device_id=device, device_id_type=MESH,
    )


def started(copies):
    for copy in copies:
        copy.start()
    return copies


def started_far_first(copies):
    count = len(copies) + 1
    for k in sorted(range(1, count), key=lambda k: -min(k, count - k)):
        copies[k - 1].start()
    return copies


class Scan:
    def __init__(self, step, src, carry, result, scratch):
        self.step, self.src, self.carry_ref, self.result = step, src, carry, result
        self.buf, self.back, self.total, self.group = scratch[:4]
        self.out_sems, self.back_sems, self.group_sems = scratch[4:6], scratch[6:8], scratch[8:10]
        self.dp, _, self.z, self.y = place()
        self.out_copies, self.back_copies = [], []
        self.order = range(NY) if step > 0 else range(NY - 1, -1, -1)

    def around(self, k):
        return lax.rem(self.y + k, NY)

    def at_y(self, k):
        return (self.dp, self.z * NY + self.around(k))

    def carry(self, j):
        return self.carry_ref[pl.ds(j, 1), :]

    def block(self, j):
        return self.buf[lax.rem(self.y - j + NY, NY)]

    def scatter(self, offsets):
        self.out_copies += started([
            send(self.src.at[self.around(k)], self.buf.at[k], self.out_sems, k, self.at_y(k))
            for k in offsets
        ])

    def group_copy(self, far):
        there = (self.dp, (self.z + self.step * far) * NY + self.y)
        return send(self.total, self.group.at[far - 1], self.group_sems, far - 1, there)

    def has(self, far):
        other = self.z + far
        return (other >= 0) & (other < NZL)

    def totals(self):
        self.buf[0] = self.src[self.y]
        for copy in self.out_copies:
            copy.wait_recv()
        total = jnp.zeros((WIDTH, WIDTH), f32)
        for j in self.order:
            total = self.carry(j) * total + self.block(j)
        self.total[...] = total
        for far in (1, 2):
            pl.when(self.has(self.step * far))(lambda far=far: self.group_copy(far).start())

    def combine(self):
        for far in (1, 2):
            source = self.has(-self.step * far)
            pl.when(source)(lambda far=far: self.group_copy(far).wait_recv())

            @pl.when(jnp.logical_not(source))
            def _():
                self.group[far - 1] = jnp.zeros((WIDTH, WIDTH), f32)

        now = self.group[0] + self.carry(8 if self.step > 0 else 9) * self.group[1]
        for j in self.order:
            self.back[j] = now
            now = self.carry(j) * now + self.block(j)

    def give_back(self, offsets):
        self.back_copies += started([
            send(self.back.at[self.around(k)], self.result.at[self.y], self.back_sems, k, self.at_y(k))
            for k in offsets
        ])

    def arrive(self, use):
        self.result[self.y] = self.back[self.y]
        use(self.y)
        for k in DIRECT:
            send(
                self.back.at[0], self.result.at[self.around(NY - k)], self.back_sems, k, self.at_y(k)
            ).wait_recv()
            use(self.around(NY - k))

    def finish(self):
        for far in (1, 2):
            pl.when(self.has(self.step * far))(lambda far=far: self.group_copy(far).wait_send())
        for copy in self.out_copies + self.back_copies:
            copy.wait_send()


FAR, NEAR = (4, 3, 5), (2, 6, 1, 7)
DIRECT = FAR + NEAR
HEADS_BUF = pltpu.VMEM((HEADS, WIDTH, WIDTH), f32)
SCAN_SCRATCH = [
    HEADS_BUF, HEADS_BUF, pltpu.VMEM((WIDTH, WIDTH), f32), pltpu.VMEM((2, WIDTH, WIDTH), f32),
] + [pltpu.SemaphoreType.DMA((NY,))] * 4 + [pltpu.SemaphoreType.DMA((2,))] * 2


def attention_block(q_ref, k_ref, v_ref, rate_ref, len_ref, attention_buf):
    base = lax.axis_index("ctx") * ROWS
    same, distance = pair_tables(base, doc_bounds(len_ref))
    for h in range(HEADS):
        cols = pl.ds(h * WIDTH, WIDTH)
        v = v_ref[:, cols]
        mask = jnp.where(same, jnp.exp(-rate_ref[h] * distance), 0.0)
        s_high, s_low = split(matmul(q_ref[:, cols], k_ref[:, cols], NT) * mask)
        attention_buf[:, cols] = matmul(s_high, v, NN) + matmul(s_low, v, NN)


def head_columns(head):
    return pl.ds(pl.multiple_of(head * WIDTH, WIDTH), WIDTH)


def attention_head(q_ref, rate_ref, tables, in_ref, attention_buf, head):
    offsets, entering, _ = tables
    cols = head_columns(head)
    q = q_ref[:, cols]
    entry = jnp.where(entering, jnp.exp(-rate_ref[head] * offsets), 0.0)
    in_high, in_low = split(in_ref[head])
    attention_buf[:, cols] += entry * (matmul(q, in_high, NN) + matmul(q, in_low, NN))


def norm_part(gain_ref, attention_buf, normed_buf):
    attention = attention_buf[...]
    mean = jnp.mean(attention * attention, axis=-1, keepdims=True)
    normed_buf[...] = (attention * lax.rsqrt(mean + norm_eps) * gain_ref[...]).astype(bf16)


def gradient_head(k_ref, v_ref, rate_ref, tables, grad_ref, dk_part, dv_part, dk_ref, dv_ref, head):
    offsets, _, leaving = tables
    cols = head_columns(head)
    k, v = k_ref[:, cols], v_ref[:, cols]
    leave = jnp.where(leaving, jnp.exp(-rate_ref[head] * (ROWS - offsets)), 0.0)
    grad_high, grad_low = split(grad_ref[head])
    dk = leave * (matmul(v, grad_high, NT) + matmul(v, grad_low, NT))
    dk_ref[:, cols] = (dk_part[:, cols] + dk).astype(bf16)
    dv = leave * (matmul(k, grad_high, NN) + matmul(k, grad_low, NN))
    dv_ref[:, cols] = (dv_part[:, cols] + dv).astype(bf16)


def hand_over(*refs):
    for src, dst in zip(refs[:len(refs) // 2], refs[len(refs) // 2:]):
        dst[...] = src[...]


def pair_tables(base, bounds):
    rows = lax.broadcasted_iota(jnp.int32, (ROWS, ROWS), 0)
    columns = lax.broadcasted_iota(jnp.int32, (ROWS, ROWS), 1)
    same = (doc_of(base + rows, bounds) == doc_of(base + columns, bounds)) & (rows >= columns)
    return same, jnp.maximum(rows - columns, 0).astype(f32)


def block_part(q_ref, k_ref, v_ref, g_ref, rate_ref, len_ref, in_ref, dq_ref, dk_ref, dv_ref):
    base = lax.axis_index("ctx") * ROWS
    bounds = doc_bounds(len_ref)
    offsets, entering, _ = edge_tables(base, bounds)
    same, distance = pair_tables(base, bounds)
    for h in range(HEADS):
        cols = pl.ds(h * WIDTH, WIDTH)
        rate = rate_ref[h]
        q, k, v, g = q_ref[:, cols], k_ref[:, cols], v_ref[:, cols], g_ref[:, cols]
        mask = jnp.where(same, jnp.exp(-rate * distance), 0.0)
        entry = jnp.where(entering, jnp.exp(-rate * offsets), 0.0)
        s_high, s_low = split(matmul(q, k, NT) * mask)
        d_high, d_low = split(matmul(g, v, NT) * mask)
        in_high, in_low = split(in_ref[h])
        dq = matmul(d_high, k, NN) + matmul(d_low, k, NN)
        dq += entry * (matmul(g, in_high, NT) + matmul(g, in_low, NT))
        dq_ref[:, cols] = dq.astype(bf16)
        dk_ref[:, cols] = matmul(d_high, q, TN) + matmul(d_low, q, TN)
        dv_ref[:, cols] = matmul(s_high, g, TN) + matmul(s_low, g, TN)


def main_kernel(
    scale, q_ref, k_ref, v_ref, g_ref, layer_ref, gain_ref, rate_ref, len_ref,
    dq_ref, dk_ref, dv_ref, out_ref,
    grad_ref, dk_part, dv_part, state_ref, pull_ref, carry_ref, in_ref, px_ref, pz_ref, attention_buf, normed_buf, cx_buf, ax_buf, x_buf, bx_buf, xz_buf, cz_buf, az_buf, z_buf, bz_buf, zx_buf, c_buf, y_buf,
    core_send, core_recv, x_send, x_recv, xz_send, xz_recv,
    z_send, z_recv, zx_send, zx_recv, y_send, y_recv, *scratch,
):
    dp, ctx, z_low, y = place()
    x, z_high, core = dp // 4, lax.rem(dp // 2, 2), lax.rem(dp, 2)
    z = z_high * 4 + z_low
    twin = (dp + 1 - 2 * core, ctx)

    def at_x(k):
        return (lax.rem(x + k, NX) * 4 + lax.rem(dp, 4), ctx)

    def at_z(k):
        there = lax.rem(z + k, NZ)
        return (x * 4 + there // 4 * 2 + core, lax.rem(there, 4) * NY + y)

    def at_y(k):
        return (dp, ctx - y + lax.rem(y + k, NY))

    ahead = Scan(1, state_ref, carry_ref, in_ref, scratch[:10])
    scan = Scan(-1, pull_ref, carry_ref, grad_ref, scratch[10:])
    partners = (
        [twin] + [at_x(k) for k in range(1, NX)] + [at_z(k) for k in range(1, NZ)]
        + [at_y(k) for k in range(1, NY)]
    )
    barrier = pltpu.get_barrier_semaphore()
    for device in partners:
        pl.semaphore_signal(barrier, inc=1, device_id=device, device_id_type=MESH)
    state_part(k_ref, v_ref, rate_ref, len_ref, state_ref, carry_ref)
    pl.semaphore_wait(barrier, len(partners))
    ahead.scatter(DIRECT)
    pull_part(q_ref, g_ref, rate_ref, len_ref, pull_ref)
    attention_block(q_ref, k_ref, v_ref, rate_ref, len_ref, attention_buf)
    ahead.totals()
    scan.scatter(NEAR)
    ahead.combine()
    ahead.give_back(DIRECT)
    scan.scatter(FAR)
    tables = edge_tables(ctx * ROWS, doc_bounds(len_ref))
    ahead.arrive(
        functools.partial(attention_head, q_ref, rate_ref, tables, in_ref, attention_buf)
    )
    norm_part(gain_ref, attention_buf, normed_buf)

    def product(block, columns):
        return matmul(normed_buf[:, head_columns(block)], layer_ref[:, columns], TN)

    for h in range(HEADS):
        rows = product(h, slice(XCOLS, None))
        for half in range(2):
            for low in range(NZL):
                row = half * 64 + low * 16
                pz_ref[h % 2 * 4 + low, half, h // 2] = rows[row:row + 16]
    core_sems = (core_send, core_recv)
    core_copies = started([send(pz_ref.at[:, 1 - core], cz_buf, core_sems, NX, twin)])

    def to_twin(k):
        there = lax.rem(x + k, NX)
        for high in range(2):
            rows = product(there * 2 + high, slice(0, XCOLS))
            for half in range(2):
                px_ref[there, high, half] = rows[half * 64:half * 64 + 64]
        core_copies.extend(
            started([send(px_ref.at[there, :, 1 - core], cx_buf.at[k], core_sems, k, twin)])
        )

    def to_z(offsets):
        return started([
            send(az_buf.at[lax.rem(z + k, NZ)], z_buf.at[k], (z_send, z_recv), k, at_z(k))
            for k in offsets
        ])

    order = tuple(range(1, NX)) + (0,)
    for k in order[:2]:
        to_twin(k)
    core_copies[0].wait_recv()
    az_buf[...] = pz_ref[:, core] + cz_buf[...]
    z_copies = to_z((3, 4, 5))
    for k in order[2:]:
        to_twin(k)
    x_copies = []
    for k, copy in zip(order, core_copies[1:]):
        copy.wait_recv()
        ax_buf[k] = px_ref[lax.rem(x + k, NX), :, core] + cx_buf[k]
        if k:
            x_copies += started([send(ax_buf.at[k], x_buf.at[k], (x_send, x_recv), k, at_x(k))])
    scan.totals()
    z_copies = to_z((1, 2)) + z_copies + to_z((6, 7))
    block_part(q_ref, k_ref, v_ref, g_ref, rate_ref, len_ref, in_ref, dq_ref, dk_part, dv_part)
    scan.combine()
    scan.give_back(DIRECT)

    def gather(total, copies, buf):
        for k, copy in enumerate(copies, 1):
            copy.wait_recv()
            total = total + buf[k]
        return total

    bx_buf[...] = gather(ax_buf[0], x_copies, x_buf).reshape(bx_buf.shape)
    xz_copies = started_far_first([
        send(bx_buf.at[lax.rem(z + k, NZ)], xz_buf.at[k], (xz_send, xz_recv), k, at_z(k))
        for k in range(1, NZ)
    ])
    bz_buf[...] = gather(az_buf[z], z_copies, z_buf)
    zx_copies = started_far_first([
        send(bz_buf.at[lax.rem(x + k, NX)], zx_buf.at[k], (zx_send, zx_recv), k, at_x(k))
        for k in range(1, NX)
    ])
    right = gather(bz_buf[x], zx_copies, zx_buf)
    left = gather(bx_buf[z], xz_copies, xz_buf)
    for j in range(NY):
        c_buf[j, :, :XCOLS] = left[2 * j:2 * j + 2, :]
        c_buf[j, :, XCOLS:] = right[2 * j:2 * j + 2, :]
    y_copies = started_far_first([
        send(c_buf.at[lax.rem(y + k, NY)], y_buf.at[k], (y_send, y_recv), k, at_y(k))
        for k in range(1, NY)
    ])
    scan.arrive(functools.partial(
        gradient_head, k_ref, v_ref, rate_ref, tables, grad_ref, dk_part, dv_part, dk_ref, dv_ref
    ))
    out_ref[...] = gather(c_buf[y], y_copies, y_buf) * scale
    scan.finish()
    ahead.finish()
    for copy in core_copies + x_copies + z_copies + xz_copies + zx_copies + y_copies:
        copy.wait_send()


def on_device(queries, keys, values, out_grad, layer_grad, norm_gain, decay_rates, doc_lengths):
    rows, features, bucket = ROWS, HEADS * WIDTH, layer_grad.shape[2]
    scale = 1.0 / math.sqrt(rows * lax.axis_size("dp") * lax.axis_size("ctx"))
    q, k, v, g = (a.reshape(rows, features) for a in (queries, keys, values, out_grad))
    layer = layer_grad.reshape(rows, bucket)
    zcols = bucket - XCOLS
    dma = pltpu.SemaphoreType.DMA
    grad_shape = jax.ShapeDtypeStruct((rows, features), bf16)
    results = (grad_shape,) * 3 + (jax.ShapeDtypeStruct((2, bucket), f32),)
    parts = pl.pallas_call(
        functools.partial(main_kernel, scale),
        out_shape=results,
        in_specs=[VMEM_SPEC] * 6 + [SMEM_SPEC] * 2,
        out_specs=(VMEM_SPEC,) * 4,
        scratch_shapes=[
            HEADS_BUF,
            pltpu.VMEM((rows, features), f32),
            pltpu.VMEM((rows, features), f32),
            HEADS_BUF,
            HEADS_BUF,
            pltpu.VMEM((16, WIDTH), f32),
            HEADS_BUF,
            pltpu.VMEM((NX, 2, 2, 64, XCOLS), f32),
            pltpu.VMEM((NZ, 2, NX, 16, zcols), f32),
            pltpu.VMEM((rows, features), f32),
            pltpu.VMEM((rows, features), bf16),
        ]
        + [pltpu.VMEM((NX, 2, 64, XCOLS), f32)] * 3
        + [pltpu.VMEM((NZ, 16, XCOLS), f32)] * 2
        + [pltpu.VMEM((NZ, NX, 16, zcols), f32)] * 3
        + [pltpu.VMEM((NX, 16, zcols), f32)] * 2
        + [pltpu.VMEM((NY, 2, bucket), f32)] * 2
        + [dma((NX + 1,))] * 2 + [dma((NX,))] * 2 + [dma((NZ,))] * 4
        + [dma((NX,))] * 2 + [dma((NY,))] * 2
        + SCAN_SCRATCH * 2,
        compiler_params=pltpu.CompilerParams(collective_id=0, has_side_effects=True),
        name="main",
    )(q, k, v, g, layer, norm_gain.reshape(1, features), decay_rates, doc_lengths)
    query_grad, key_grad, value_grad, proj_grad = pl.pallas_call(
        hand_over,
        out_shape=results,
        in_specs=[VMEM_SPEC] * 4,
        out_specs=(VMEM_SPEC,) * 4,
        name="results",
    )(*parts)
    shape_out = (1, rows, features)
    return (
        query_grad.reshape(shape_out),
        key_grad.reshape(shape_out),
        value_grad.reshape(shape_out),
        proj_grad,
    )


def solution(mesh):
    block = P("dp", "ctx", None)
    return jax.shard_map(
        on_device,
        mesh=mesh,
        in_specs=(block,) * 5 + (P(), P(), P("dp", None)),
        out_specs=(block,) * 3 + (P(("dp", "ctx"), None),),
        check_vma=False,
    )
```
